128 devices in a mesh: draw: 8 (over z_lo, y), width: 8 (over x, core), cores: 2 (over z_hi).
Axes of the slice: x: 4, y: 4, z: 4 (z_hi: 2, z_lo: 2; z = z_hi * 2 + z_lo), core: 2. Of those that a mesh axis runs over, the one named last changes fastest.
Arguments:
- warmth_history: float32 [10, 4096, 2048], P(None, ('draw', 'width', 'cores')), may hold values from 0.9 to 1.1
- fictitious_warmth: float32 [4096, 2048], P('draw', ('width', 'cores')), may hold values from 0.9 to 1.1
- vertex_velocity: float32 [2, 4096, 2048], P(None, 'draw', ('width', 'cores')), may hold values from -6 to 6
- branch_load_tensors: float32 [12, 3, 4096, 2048], P(None, None, 'draw', ('width', 'cores')), may hold values from -2 to 2
- mechanism_lifetimes: float32 [12], replicated, may hold values from 0.3 to 30
- branch_stiffness: float32 [12], replicated, may hold values from 0.005 to 0.025
Outputs:
- fictive_final: float32 [4096, 2048], P('draw', ('width', 'cores'))
- velocity_final: float32 [2, 4096, 2048], P(None, 'draw', ('width', 'cores'))
- modes_final: float32 [12, 3, 4096, 2048], P(None, None, 'draw', ('width', 'cores'))
The draws below stay inside these ranges and needn't reach their ends.
All inputs are finite; a program needn't handle non-finite values.
Results may differ from the reference program's by a relative error of at most 0.0001.
Values sent between devices are 32-bit elements; how exact they have to be, the bound alone decides.
No kernel may reach another device: no remote copies, remote signals or barrier semaphores. Data moves between devices by JAX's collectives and lax.ppermute only.
A program may use at most 128 MiB of HBM per device.

```python
import math
import jax
import jax.numpy as jnp
from jax import lax

MODES = 12
HORIZON_TICKS = 10
AXIAL_CELLS = 4096
LATERAL_CELLS = 2048


def block_scale(rng, extent, cuts, low, high):
    loudness, own = 1.0, jax.random.fold_in(rng, 6)
    for position, parts in cuts:
        steps = jnp.exp(jax.random.uniform(jax.random.fold_in(own, position), (parts,), jnp.float32, low / len(cuts), high / len(cuts)))
        loudness = loudness * jnp.repeat(steps, extent[position] // parts).reshape([-1 if axis == position else 1 for axis in range(len(extent))])
    return loudness


def bell_draw(key, shape, scale, limit, cuts=(), held_as=jnp.bfloat16):
    values = jax.random.normal(key, shape, jnp.float32) * scale
    if len(cuts) > 0:
        values = block_scale(key, shape, cuts, -0.22, 0.18) * values
    return jnp.clip(values, min=-limit, max=limit).astype(held_as)


def setup_inputs(seed: int = 0) -> dict:
    seeds = jax.random.split(jax.random.key(seed), 7)
    return {
        "warmth_history": jnp.clip(0.9 + 0.20000005 * jax.random.uniform(seeds[0], (HORIZON_TICKS, AXIAL_CELLS, LATERAL_CELLS), jnp.float32) ** block_scale(seeds[0], (HORIZON_TICKS, AXIAL_CELLS, LATERAL_CELLS), ((1, 128),), -0.2, 0.2), 0.9, 1.1),
        "fictitious_warmth": jnp.clip(0.9 + 0.20000005 * jax.random.uniform(seeds[1], (AXIAL_CELLS, LATERAL_CELLS), jnp.float32) ** block_scale(seeds[1], (AXIAL_CELLS, LATERAL_CELLS), ((0, 8), (1, 16)), -0.2, 0.2), 0.9, 1.1),
        "vertex_velocity": bell_draw(seeds[2], (2, AXIAL_CELLS, LATERAL_CELLS), 1.0, 6.0, ((1, 8), (2, 16)), jnp.float32),
        "branch_load_tensors": bell_draw(seeds[3], (MODES, 3, AXIAL_CELLS, LATERAL_CELLS), 0.2, 2.0, ((2, 8), (3, 16)), jnp.float32),
        "mechanism_lifetimes": jnp.clip(jnp.exp(jax.random.uniform(seeds[4], (MODES,), jnp.float32, math.log(0.3), math.log(30.0))), 0.3, 30.0),
        "branch_stiffness": jnp.clip(jnp.exp(jax.random.uniform(seeds[5], (MODES,), jnp.float32, math.log(0.005), math.log(0.025))), 0.005, 0.025),
    }


clock_increment = 1.0
arrhenius_energy = 20.0
coupling_exponent = 0.5
reduced_clock = 3.0


def strain_field(motion):
    padded = jnp.pad(motion, ((0, 0), (0, 1), (0, 1)))
    below = padded[:, 1:, :-1]
    beside = padded[:, :-1, 1:]
    corner = padded[:, 1:, 1:]
    grad_len = 0.5 * ((below + corner) - (motion + beside))
    grad_wid = 0.5 * ((beside + corner) - (motion + below))
    return jnp.stack([grad_len[0], grad_wid[1], 0.5 * (grad_wid[0] + grad_len[1])])


def nodal_field(stress):
    along_len = -0.5 * jnp.stack([stress[0], stress[2]])
    along_wid = -0.5 * jnp.stack([stress[2], stress[1]])
    node_base = -along_len - along_wid
    node_down = along_len - along_wid
    node_right = along_wid - along_len
    node_diag = along_len + along_wid
    width_pad = ((0, 0), (0, 0), (1, 0))
    row_here = node_base + jnp.pad(node_right, width_pad)[:, :, :-1]
    row_next = node_down + jnp.pad(node_diag, width_pad)[:, :, :-1]
    return row_here + jnp.pad(row_next, ((0, 0), (1, 0), (0, 0)))[:, :-1, :]


def relax_mode(stress_mode, relax_time, modulus, strain, multiplier):
    rate_ratio = clock_increment / (relax_time * multiplier)
    kept = jnp.exp(-rate_ratio)
    weight = -jnp.expm1(-rate_ratio) / rate_ratio
    return kept * stress_mode + (2.0 * clock_increment * modulus) * weight * strain


def reference(warmth_history, fictitious_warmth, vertex_velocity, branch_load_tensors, mechanism_lifetimes, branch_stiffness):
    for locator_now in range(HORIZON_TICKS):
        warmth_now = warmth_history[locator_now]
        warming_contribution = arrhenius_energy * coupling_exponent / warmth_now - arrhenius_energy
        multiplier = jnp.exp(warming_contribution + arrhenius_energy * (1.0 - coupling_exponent) / fictitious_warmth)
        fictitious_warmth = warmth_now + (fictitious_warmth - warmth_now) * jnp.exp(-clock_increment / (reduced_clock * multiplier))
        strain = strain_field(vertex_velocity)

        def update_one(packed):
            return relax_mode(packed[0], packed[1], packed[2], strain, multiplier)

        branch_load_tensors = lax.map(update_one, (branch_load_tensors, mechanism_lifetimes, branch_stiffness))
        stress = jnp.sum(branch_load_tensors, axis=0)
        vertex_velocity = vertex_velocity + clock_increment * nodal_field(stress)
    return fictitious_warmth, vertex_velocity, branch_load_tensors
```

```python
import jax
import jax.numpy as jnp
from jax import lax
from jax.experimental import pallas as pl
from jax.experimental.pallas import tpu as pltpu
from jax.sharding import PartitionSpec as P

LOG2E = 1.4426950408889634
OUTSIDE = -1.0 / 3.0
TICKS = 10
MODES = 12
PIECES = 16
ROWS = 512
COLS = 128
HALO = 16
EXT = ROWS + 2 * HALO
DEEP = 10
LANES = 640
SUBS = 24
BLK = 32
F32 = jnp.float32
VMEM = pltpu.VMEM
ANY = pl.ANY
SMEM = pltpu.SMEM
WIDE = ("width", "cores")


def shifted(shard, axis, by):
    peers = lax.axis_size(axis)
    pairs = [(i, i + by) for i in range(peers) if 0 <= i + by < peers]
    return lax.ppermute(shard, axis, pairs)


def params(mb):
    return pltpu.CompilerParams(vmem_limit_bytes=mb << 20)


def iota(shape, axis):
    return lax.broadcasted_iota(jnp.int32, shape, axis)


def pack_heat_body(src, dst, buf, side, in_sem, out_sem, side_sem):
    def fetch(p):
        return pltpu.make_async_copy(src.at[:, :, pl.ds(p * COLS, COLS)], buf.at[p], in_sem.at[p])

    def put(p):
        return pltpu.make_async_copy(buf.at[p], dst.at[p, pl.ds(0, TICKS)], out_sem.at[p])

    def put_side(p):
        return pltpu.make_async_copy(side.at[p], dst.at[p, TICKS], side_sem.at[p])

    for p in range(PIECES):
        fetch(p).start()
    lane = iota((32, COLS), 1)
    for p in range(PIECES):
        fetch(p).wait()
        put(p).start()
        if p == 0:
            side[0] = jnp.full((32, COLS), OUTSIDE, F32)
            put_side(0).start()
        if p + 1 < PIECES:
            acc = jnp.full((32, COLS), 1.0, F32)
            for n in range(TICKS):
                moved = pltpu.roll(buf[p, n], (DEEP * n + DEEP) % COLS, 1)
                acc = jnp.where((lane >= DEEP * n) & (lane < DEEP * n + DEEP), moved, acc)
            side[p + 1] = acc
            put_side(p + 1).start()
    for p in range(PIECES):
        put(p).wait()
        put_side(p).wait()


def pack_heat(slab):
    return pl.pallas_call(
        pack_heat_body,
        out_shape=jax.ShapeDtypeStruct((PIECES, TICKS + 1, 32, COLS), F32),
        in_specs=[pl.BlockSpec(memory_space=ANY)],
        out_specs=pl.BlockSpec(memory_space=ANY),
        scratch_shapes=[
            VMEM((PIECES, TICKS, 32, COLS), F32),
            VMEM((PIECES, 32, COLS), F32),
            pltpu.SemaphoreType.DMA((PIECES,)),
            pltpu.SemaphoreType.DMA((PIECES,)),
            pltpu.SemaphoreType.DMA((PIECES,)),
        ],
        compiler_params=params(16),
        name="pack_heat",
    )(slab)


def turned(own, up, down, fill):
    last = jnp.concatenate([down, jnp.full((COLS - 2 * HALO, COLS), fill, F32), up], axis=0)
    return jnp.concatenate([own[i * COLS:(i + 1) * COLS].T for i in range(4)] + [last.T], axis=1)


def pack_state_body(flags, s_ref, vf_v, vf_f, up, down, first, last):
    i = pl.program_id(0)

    def edges(blocks):
        return (jnp.concatenate([b[:DEEP] for b in blocks], axis=0),
                jnp.concatenate([b[COLS - DEEP:] for b in blocks], axis=0))

    blocks = [turned(s_ref[q], up[4 * i + q], down[4 * i + q], 0.0) for q in range(4)]
    a, b = edges(blocks)
    at = pl.multiple_of(i * 40, 8)
    first[pl.ds(at, 40), :] = a
    last[pl.ds(at, 40), :] = b

    @pl.when(i == 8)
    def _():
        f_up = jnp.where(flags[0] == 1, OUTSIDE, up[38])
        f_down = jnp.where(flags[1] == 1, OUTSIDE, down[38])
        rest = [turned(vf_v[0], up[36], down[36], 0.0), turned(vf_v[1], up[37], down[37], 0.0),
                turned(vf_f[...], f_up, f_down, 1.0)]
        a, b = edges(rest)
        pad = jnp.zeros((2, LANES), F32)
        first[360:392, :] = jnp.concatenate([a, pad], axis=0)
        last[360:392, :] = jnp.concatenate([b, pad], axis=0)


def pack_state(flags, state, motion, fictive, up, down):
    whole = lambda shape: pl.BlockSpec(shape, lambda i: (0,) * len(shape))
    return pl.pallas_call(
        pack_state_body,
        out_shape=[jax.ShapeDtypeStruct((392, LANES), F32)] * 2,
        grid=(9,),
        in_specs=[
            pl.BlockSpec(memory_space=SMEM),
            pl.BlockSpec((4, ROWS, COLS), lambda i: (i, 0, 0)),
            whole((2, ROWS, COLS)),
            whole((ROWS, COLS)),
            whole((39, HALO, COLS)),
            whole((39, HALO, COLS)),
        ],
        out_specs=[whole((392, LANES))] * 2,
        compiler_params=params(32),
        name="pack_state",
    )(flags, state, motion, fictive, up, down)


def shift_of(theta, fict):
    arg = 10.0 * (theta + fict) / (theta * fict) - 20.0
    inv = jnp.exp(-arg)
    return inv, jnp.exp(arg)


def strip_body(flags, coef, first, got, heat, heat_up, heat_down, sigma, nodes, z, v, q, heat_t):
    for k in range(36):
        z[k, 0:DEEP, :] = got[DEEP * k:DEEP * k + DEEP, :]
        z[k, DEEP:2 * DEEP, :] = first[DEEP * k:DEEP * k + DEEP, :]
        z[k, 2 * DEEP:SUBS, :] = jnp.zeros((SUBS - 2 * DEEP, LANES), F32)
    for k in range(2):
        at = 360 + DEEP * k
        v[k, 0:DEEP, :] = got[at:at + DEEP, :]
        v[k, DEEP:2 * DEEP, :] = first[at:at + DEEP, :]
        v[k, 2 * DEEP:SUBS, :] = jnp.zeros((SUBS - 2 * DEEP, LANES), F32)
    f_left = jnp.where(flags[2] == 1, OUTSIDE, got[380:390, :])
    ones = jnp.ones((SUBS - 2 * DEEP, LANES), F32)
    fict0 = jnp.concatenate([f_left, first[380:390, :], ones], axis=0)
    q[...] = jnp.zeros((3, SUBS, LANES), F32)

    top, bottom = flags[0] == 1, flags[1] == 1
    side = turned(heat[:, TICKS].reshape(ROWS, COLS), jnp.where(top, OUTSIDE, heat_up[TICKS]),
                  jnp.where(bottom, OUTSIDE, heat_down[TICKS]), 1.0)

    def gathered(pick, rows):
        lane = iota((rows, COLS), 1)
        acc = jnp.full((rows, COLS), 1.0, F32)
        for n in range(TICKS):
            moved = pltpu.roll(pick(n), DEEP * n, 1) if n else pick(n)
            acc = jnp.where((lane >= DEEP * n) & (lane < DEEP * n + DEEP), moved, acc)
        return acc

    own = jnp.concatenate([gathered(lambda n: heat[s, n], 32) for s in range(PIECES)], axis=0)
    mine = turned(own, gathered(lambda n: jnp.where(top, OUTSIDE, heat_up[n]), HALO),
                  gathered(lambda n: jnp.where(bottom, OUTSIDE, heat_down[n]), HALO), 1.0)
    for n in range(TICKS):
        heat_t[n, 0:DEEP, :] = side[DEEP * n:DEEP * n + DEEP]
        heat_t[n, DEEP:2 * DEEP, :] = mine[DEEP * n:DEEP * n + DEEP]
        heat_t[n, 2 * DEEP:SUBS, :] = ones

    lane = iota((SUBS, LANES), 1)
    inside = jnp.where(bottom & (lane >= ROWS) & (lane < LANES - HALO), 0.0, 1.0)
    sum_a = coef[24]

    def tick(n, fict):
        theta = heat_t[n]
        inv, shift = shift_of(theta, fict)
        fict_next = theta + (fict - theta) * jnp.exp(inv * (-1.0 / 3.0))

        def grads(m):
            beside = pltpu.roll(m, SUBS - 1, 0)
            both, diff = m + beside, beside - m
            along = 0.5 * (pltpu.roll(both, LANES - 1, 1) - both)
            across = 0.5 * (pltpu.roll(diff, LANES - 1, 1) + diff)
            return along, across

        u, w = v[0], v[1]
        nodes[pl.ds(n, 1), :] = u[DEEP:DEEP + 1]
        nodes[pl.ds(16 + n, 1), :] = w[DEEP:DEEP + 1]
        lu, wu = grads(u)
        lw, ww = grads(w)
        now = [shift * lu, shift * ww, shift * (0.5 * (wu + lw))]
        delta = [q[c] - now[c] for c in range(3)]
        for c in range(3):
            q[c] = now[c]
        total = [sum_a * now[c] for c in range(3)]
        for k in range(MODES):
            kept = jnp.exp2(inv * coef[k])
            a = coef[12 + k]
            for c in range(3):
                new = kept * (z[3 * k + c] + a * delta[c])
                z[3 * k + c] = new
                total[c] = total[c] + new
        for c in range(3):
            sigma[pl.ds(16 * c + n, 1), :] = total[c][DEEP - 1:DEEP]

        def force(lin, cross):
            x = lin + pltpu.roll(lin, 1, 0)
            y = cross - pltpu.roll(cross, 1, 0)
            return 0.5 * ((x + y) - pltpu.roll(x - y, 1, 1))

        v[0] = (u + force(total[0], total[2])) * inside
        v[1] = (w + force(total[2], total[1])) * inside
        return fict_next

    sigma[...] = jnp.zeros((48, LANES), F32)
    nodes[...] = jnp.zeros((32, LANES), F32)
    lax.fori_loop(0, TICKS, tick, fict0)


def strip(flags, coef, first, got, heat, heat_up, heat_down):
    full = pl.BlockSpec(memory_space=VMEM)
    smem = pl.BlockSpec(memory_space=SMEM)
    return pl.pallas_call(
        strip_body,
        out_shape=[jax.ShapeDtypeStruct((48, LANES), F32), jax.ShapeDtypeStruct((32, LANES), F32)],
        in_specs=[smem, smem] + [full] * 5,
        out_specs=[full, full],
        scratch_shapes=[
            VMEM((36, SUBS, LANES), F32),
            VMEM((2, SUBS, LANES), F32),
            VMEM((3, SUBS, LANES), F32),
            VMEM((TICKS, SUBS, LANES), F32),
        ],
        compiler_params=params(40),
        name="strip",
    )(flags, coef, first, got, heat, heat_up, heat_down)


def block_body(flags, coef, state, motion, fictive, up, down, heat, heat_up, heat_down, sigma, nodes,
               f_out, v_out, s_out, z, v, q, f, th, h, carry, z_sem, th_sem, out_sem):
    copies = []
    for k in range(36):
        copies.append(pltpu.make_async_copy(state.at[k], z.at[k, pl.ds(HALO, ROWS)], z_sem.at[k]))
    for s in range(PIECES):
        copies.append(pltpu.make_async_copy(heat.at[s, pl.ds(0, TICKS)], th.at[:, s + 1], th_sem.at[s]))
    for c in copies:
        c.start()
    top, bottom = flags[0] == 1, flags[1] == 1
    for k in range(36):
        z[k, 0:HALO, :] = up[k]
        z[k, HALO + ROWS:EXT, :] = down[k]
    for c in range(2):
        v[c, 0:HALO, :] = up[36 + c]
        v[c, HALO:HALO + ROWS, :] = motion[c]
        v[c, HALO + ROWS:EXT, :] = down[36 + c]
        v[c, EXT:EXT + 8, :] = jnp.zeros((8, COLS), F32)
    f[0:HALO, :] = jnp.where(top, OUTSIDE, up[38])
    f[HALO:HALO + ROWS, :] = fictive[...]
    f[HALO + ROWS:EXT, :] = jnp.where(bottom, OUTSIDE, down[38])
    for n in range(TICKS):
        th[n, 0, HALO:BLK, :] = jnp.where(top, OUTSIDE, heat_up[n])
        th[n, PIECES + 1, 0:HALO, :] = jnp.where(bottom, OUTSIDE, heat_down[n])
    q[...] = jnp.zeros((3, EXT, COLS), F32)
    pad = jnp.zeros((COLS - 80, COLS), F32)
    for i in range(5):
        part = jnp.concatenate([sigma[:, i * COLS:(i + 1) * COLS], nodes[:, i * COLS:(i + 1) * COLS], pad], axis=0).T
        if i < 4:
            h[HALO + i * COLS:HALO + (i + 1) * COLS, :] = part
        else:
            h[HALO + ROWS:EXT, :] = part[0:HALO]
            h[0:HALO, :] = part[COLS - HALO:]
            h[EXT:EXT + 8, :] = jnp.zeros((8, COLS), F32)
    for c in copies:
        c.wait()

    lane_v = iota((BLK + 8, COLS), 1)
    lane_s = iota((BLK, COLS), 1)
    row_8 = iota((8, COLS), 0)
    sum_a = coef[24]

    def tick(n, last):
        to_right = lax.rem(127 - 48 - n + COLS, COLS)
        carry[...] = jnp.zeros((2, 8, COLS), F32)

        def rows(b, _):
            r0 = pl.multiple_of(b * BLK, BLK)
            at = pl.ds(r0, BLK)
            j = 2 * b + 1
            theta = jnp.concatenate([th[n, b, HALO:BLK, :], th[n, b + 1, 0:HALO, :]], axis=0)
            fict = f[at, :]
            inv, shift = shift_of(theta, fict)
            f[at, :] = theta + (fict - theta) * jnp.exp(inv * (-1.0 / 3.0))
            hist = h[pl.ds(r0, BLK + 8), :]

            def grads(m, to):
                beside = jnp.where(lane_v == COLS - 1, pltpu.roll(hist, to, 1), pltpu.roll(m, COLS - 1, 1))
                both, diff = m + beside, beside - m
                along = 0.5 * (both[1:BLK + 1] - both[:BLK])
                across = 0.5 * (diff[1:BLK + 1] + diff[:BLK])
                return along, across

            u, w = v[0, pl.ds(r0, BLK + 8), :], v[1, pl.ds(r0, BLK + 8), :]
            lu, wu = grads(u, to_right)
            lw, ww = grads(w, lax.rem(to_right + COLS - 16, COLS))
            now = [shift * lu, shift * ww, shift * (0.5 * (wu + lw))]
            delta = [q[c, at, :] - now[c] for c in range(3)]
            for c in range(3):
                q[c, at, :] = now[c]
            total = [sum_a * now[c] for c in range(3)]
            for k in range(MODES):
                kept = jnp.exp2(inv * coef[k])
                a = coef[12 + k]
                for c in range(3):
                    new = kept * (z[3 * k + c, at, :] + a * delta[c])
                    z[3 * k + c, at, :] = (new + a * now[c]) if last else new
                    total[c] = total[c] + new
            hist_s = hist[:BLK]

            def left(c):
                to = lax.rem(COLS - 16 * c - n + COLS, COLS)
                return jnp.where(lane_s == 0, pltpu.roll(hist_s, to, 1), pltpu.roll(total[c], 1, 1))

            xx_l, yy_l, xy_l = left(0), left(1), left(2)

            def force(lin, lin_l, cross, cross_l, c):
                x, y = lin + lin_l, cross - cross_l
                rolled = pltpu.roll(x - y, 1, 0)
                head = jnp.where(row_8 == 0, carry[c], rolled[:8])
                carry[c] = rolled[:8]
                return 0.5 * ((x + y) - jnp.concatenate([head, rolled[8:]], axis=0))

            v[0, at, :] = u[:BLK] + force(total[0], xx_l, total[2], xy_l, 0)
            v[1, at, :] = w[:BLK] + force(total[2], xy_l, total[1], yy_l, 1)
            return 0

        lax.fori_loop(0, EXT // BLK, rows, 0)

        @pl.when(bottom)
        def _():
            v[:, HALO + ROWS:EXT, :] = jnp.zeros((2, HALO, COLS), F32)

    def step(n, _):
        tick(n, False)
        return 0

    lax.fori_loop(0, TICKS - 1, step, 0)
    tick(TICKS - 1, True)
    outs = [pltpu.make_async_copy(z.at[k, pl.ds(HALO, ROWS)], s_out.at[k], out_sem.at[k]) for k in range(36)]
    for c in outs:
        c.start()
    f_out[...] = f[HALO:HALO + ROWS, :]
    for c in range(2):
        v_out[c] = v[c, HALO:HALO + ROWS, :]
    for c in outs:
        c.wait()


def block(flags, coef, state, motion, fictive, up, down, heat, heat_up, heat_down, sigma, nodes):
    full = pl.BlockSpec(memory_space=VMEM)
    smem = pl.BlockSpec(memory_space=SMEM)
    hbm = pl.BlockSpec(memory_space=ANY)
    return pl.pallas_call(
        block_body,
        out_shape=[
            jax.ShapeDtypeStruct((ROWS, COLS), F32),
            jax.ShapeDtypeStruct((2, ROWS, COLS), F32),
            jax.ShapeDtypeStruct((36, ROWS, COLS), F32),
        ],
        in_specs=[smem, smem, hbm, full, full, full, full, hbm, full, full, full, full],
        out_specs=[full, full, hbm],
        scratch_shapes=[
            VMEM((36, EXT, COLS), F32),
            VMEM((2, EXT + 8, COLS), F32),
            VMEM((3, EXT, COLS), F32),
            VMEM((EXT, COLS), F32),
            VMEM((TICKS, PIECES + 2, BLK, COLS), F32),
            VMEM((EXT + 8, COLS), F32),
            VMEM((2, 8, COLS), F32),
            pltpu.SemaphoreType.DMA((36,)),
            pltpu.SemaphoreType.DMA((PIECES,)),
            pltpu.SemaphoreType.DMA((36,)),
        ],
        compiler_params=params(48),
        name="block",
    )(flags, coef, state, motion, fictive, up, down, heat, heat_up, heat_down, sigma, nodes)


def shards(warmth_history, fictitious_warmth, vertex_velocity, branch_load_tensors, mechanism_lifetimes, branch_stiffness):
    state = branch_load_tensors.reshape(3 * MODES, ROWS, COLS)
    weight = 2.0 * branch_stiffness * mechanism_lifetimes
    coef = jnp.concatenate([-LOG2E / mechanism_lifetimes, weight, jnp.sum(weight)[None]])
    draw, wide = lax.axis_index("draw"), lax.axis_index(WIDE)
    flags = jnp.stack([draw == 0, draw == lax.axis_size("draw") - 1, wide == 0]).astype(jnp.int32)

    heat = lax.all_to_all(pack_heat(warmth_history), WIDE, split_axis=0, concat_axis=0, tiled=True)

    def rows_of(at):
        cut = lambda x: lax.slice_in_dim(x, at, at + HALO, axis=1)
        return jnp.concatenate([cut(state), cut(vertex_velocity), cut(fictitious_warmth[None])], axis=0)

    up = shifted(rows_of(ROWS - HALO), "draw", 1)
    down = shifted(rows_of(0), "draw", -1)
    first, final = pack_state(flags, state, vertex_velocity, fictitious_warmth, up, down)
    got = shifted(final, WIDE, 1)

    heat_up = shifted(heat[PIECES - 1, :, HALO:, :], "draw", 1)
    heat_down = shifted(heat[0, :, :HALO, :], "draw", -1)
    sigma, nodes = strip(flags, coef, first, got, heat, heat_up, heat_down)
    nodes = shifted(nodes, WIDE, -1)
    fict, motion, modes = block(flags, coef, state, vertex_velocity, fictitious_warmth, up, down, heat, heat_up, heat_down, sigma, nodes)
    return fict, motion, modes.reshape(branch_load_tensors.shape)


def solution(mesh):
    in_specs = (
        P(None, ("draw", "width", "cores"), None),
        P("draw", ("width", "cores")),
        P(None, "draw", ("width", "cores")),
        P(None, None, "draw", ("width", "cores")),
        P(),
        P(),
    )
    out_specs = (
        P("draw", ("width", "cores")),
        P(None, "draw", ("width", "cores")),
        P(None, None, "draw", ("width", "cores")),
    )
    return jax.shard_map(shards, mesh=mesh, in_specs=in_specs, out_specs=out_specs, check_vma=False)
```

```python
import jax
import jax.numpy as jnp
from jax import lax
from jax.experimental import pallas as pl
from jax.experimental.pallas import tpu as pltpu
from jax.sharding import PartitionSpec as P

LOG2E = 1.4426950408889634
OUTSIDE = -1.0 / 3.0
TICKS = 10
MODES = 12
PIECES = 16
ROWS = 512
COLS = 128
HALO = 16
EXT = ROWS + 2 * HALO
DEEP = 10
LANES = 640
SUBS = 24
PAD = 8
SUB = 16
FLOW = 272
F32 = jnp.float32
VMEM = pltpu.VMEM
ANY = pl.ANY
SMEM = pltpu.SMEM
WIDE = ("width", "cores")


def shifted(shard, axis, by):
    peers = lax.axis_size(axis)
    pairs = [(i, i + by) for i in range(peers) if 0 <= i + by < peers]
    return lax.ppermute(shard, axis, pairs)


def params(mb):
    return pltpu.CompilerParams(vmem_limit_bytes=mb << 20)


def iota(shape, axis):
    return lax.broadcasted_iota(jnp.int32, shape, axis)


def pinned(x):
    return pltpu.with_memory_space_constraint(x, pltpu.HBM)


def cut_body(src, state, motion, fictive, dst, above, below, buf, side, halo, in_sem, out_sem, side_sem, row_sem):
    def fetch(p):
        return pltpu.make_async_copy(src.at[:, :, pl.ds(p * COLS, COLS)], buf.at[p], in_sem.at[p])

    def put(p):
        return pltpu.make_async_copy(buf.at[p], dst.at[p, pl.ds(0, TICKS)], out_sem.at[p])

    def put_side(p):
        return pltpu.make_async_copy(side.at[p], dst.at[p, TICKS], side_sem.at[p])

    ins, outs = [], []
    for i, (to, at) in enumerate(((above, ROWS - HALO), (below, 0))):
        part = pl.ds(at, HALO)
        for x, y in ((state.at[:, part], pl.ds(0, 36)), (motion.at[:, part], pl.ds(36, 2)), (fictive.at[part], 38)):
            ins.append(pltpu.make_async_copy(x, halo.at[i, y], row_sem.at[len(ins)]))
        outs.append(pltpu.make_async_copy(halo.at[i], to, row_sem.at[6 + i]))
    for p in range(PIECES):
        fetch(p).start()
    for c in ins:
        c.start()
    lane = iota((32, COLS), 1)
    for p in range(PIECES):
        fetch(p).wait()
        put(p).start()
        if p == 0:
            side[0] = jnp.full((32, COLS), OUTSIDE, F32)
            put_side(0).start()
        if p + 1 < PIECES:
            acc = jnp.full((32, COLS), 1.0, F32)
            for n in range(TICKS):
                moved = pltpu.roll(buf[p, n], (DEEP * n + DEEP) % COLS, 1)
                acc = jnp.where((lane >= DEEP * n) & (lane < DEEP * n + DEEP), moved, acc)
            side[p + 1] = acc
            put_side(p + 1).start()
    for c in ins:
        c.wait()
    for c in outs:
        c.start()
    for p in range(PIECES):
        put(p).wait()
        put_side(p).wait()
    for c in outs:
        c.wait()


def cut(slab, state, motion, fictive):
    hbm = pl.BlockSpec(memory_space=pltpu.HBM)
    halo = pltpu.HBM((39, HALO, COLS), F32)
    return pl.pallas_call(
        cut_body,
        out_shape=[pltpu.HBM((PIECES, TICKS + 1, 32, COLS), F32), halo, halo],
        in_specs=[hbm] * 4,
        out_specs=[hbm] * 3,
        scratch_shapes=[
            VMEM((PIECES, TICKS, 32, COLS), F32),
            VMEM((PIECES, 32, COLS), F32),
            VMEM((2, 39, HALO, COLS), F32),
            pltpu.SemaphoreType.DMA((PIECES,)),
            pltpu.SemaphoreType.DMA((PIECES,)),
            pltpu.SemaphoreType.DMA((PIECES,)),
            pltpu.SemaphoreType.DMA((8,)),
        ],
        compiler_params=params(8),
        name="cut",
    )(pinned(slab), pinned(state), pinned(motion), pinned(fictive))


def corner(up, down, fill):
    return jnp.concatenate([down, jnp.full((COLS - 2 * HALO, COLS), fill, F32), up], axis=0).T


def turned(own):
    return jnp.concatenate([own[i * COLS:(i + 1) * COLS].T for i in range(4)], axis=1)


def pack_own_body(state, motion, fictive, first, last, buf, sem):
    copies = [pltpu.make_async_copy(state.at[pl.ds(4 * i, 4)], buf.at[pl.ds(4 * i, 4)], sem.at[i]) for i in range(9)]
    for c in copies:
        c.start()
    rest = [turned(motion[0]), turned(motion[1]), turned(fictive[...])]
    put_rest(rest, first, last)
    for i in range(9):
        copies[i].wait()
        put_state(i, [turned(buf[4 * i + q]) for q in range(4)], first, last)


def put_rest(rest, first, last):
    first[360:400, :] = jnp.concatenate([rest[0][:16], rest[1][:16], rest[2][:8]], axis=0)
    first[400:408, :] = rest[2][8:16]
    last[360:392, :] = jnp.concatenate([r[COLS - DEEP:] for r in rest] + [rest[0][:2]], axis=0)


def put_state(i, blocks, first, last):
    first[40 * i:40 * i + 40, :] = jnp.concatenate([b[:DEEP] for b in blocks], axis=0)
    last[40 * i:40 * i + 40, :] = jnp.concatenate([b[COLS - DEEP:] for b in blocks], axis=0)


def pack_own(state, motion, fictive):
    full = pl.BlockSpec(memory_space=VMEM)
    return pl.pallas_call(
        pack_own_body,
        out_shape=[jax.ShapeDtypeStruct((408, ROWS), F32), jax.ShapeDtypeStruct((392, ROWS), F32)],
        in_specs=[pl.BlockSpec(memory_space=pltpu.HBM), full, full],
        out_specs=[full] * 2,
        scratch_shapes=[VMEM((36, ROWS, COLS), F32), pltpu.SemaphoreType.DMA((9,))],
        compiler_params=params(20),
        name="pack_own",
    )(pinned(state), motion, fictive)


def pack_halo_body(flags, up, down, first, dense, last):
    f_up = jnp.where(flags[0] == 1, OUTSIDE, up[38])
    f_down = jnp.where(flags[1] == 1, OUTSIDE, down[38])
    put_rest([corner(up[36], down[36], 0.0), corner(up[37], down[37], 0.0), corner(f_up, f_down, 1.0)], first, last)
    for i in range(9):
        put_state(i, [corner(up[4 * i + q], down[4 * i + q], 0.0) for q in range(4)], first, last)
    last[392:416, :] = jnp.zeros((24, COLS), F32)
    lane = iota((104, COLS), 1)
    acc = jnp.zeros((104, COLS), F32)
    for g in range(4):
        moved = pltpu.roll(last[104 * g:104 * g + 104, :], (HALO + 32 * g) % COLS, 1)
        acc = jnp.where((lane >= 32 * g) & (lane < 32 * g + 32), moved, acc)
    dense[...] = acc


def spread(dense):
    return jnp.concatenate([pltpu.roll(dense, COLS - HALO - 32 * g, 1) for g in range(4)], axis=0)


def pack_halo(flags, up, down):
    full = pl.BlockSpec(memory_space=VMEM)
    return pl.pallas_call(
        pack_halo_body,
        out_shape=[jax.ShapeDtypeStruct((408, COLS), F32), jax.ShapeDtypeStruct((104, COLS), F32)],
        in_specs=[pl.BlockSpec(memory_space=SMEM), full, full],
        out_specs=[full] * 2,
        scratch_shapes=[VMEM((416, COLS), F32)],
        compiler_params=params(8),
        name="pack_halo",
    )(flags, up, down)


def shift_of(theta, fict):
    arg = 10.0 * (theta + fict) / (theta * fict) - 20.0
    inv = jnp.exp(-arg)
    return inv, jnp.exp(arg)


def work(us):
    return pl.CostEstimate(flops=0, transcendentals=0, bytes_accessed=us * 3_000_000)


def beside_each_other(pick, rows):
    lane = iota((rows, COLS), 1)
    acc = jnp.full((rows, COLS), 1.0, F32)
    for n in range(TICKS):
        moved = pltpu.roll(pick(n), DEEP * n, 1) if n else pick(n)
        acc = jnp.where((lane >= DEEP * n) & (lane < DEEP * n + DEEP), moved, acc)
    return acc


def advance(theta, fict):
    inv, shift = shift_of(theta, fict)
    return inv, 0.5 * shift, theta + (fict - theta) * jnp.exp(inv * (-1.0 / 3.0))


def ready_body(heat, fictive, inv_ref, half_ref, f_out, mine, side):
    def piece(s, _):
        at = pl.ds(pl.multiple_of(32 * s, 32), 32)
        to = pl.ds(pl.multiple_of(32 * s + HALO, 16), 32)
        fict = fictive[at, :]
        for n in range(TICKS):
            inv_ref[n, to, :], half_ref[n, to, :], fict = advance(heat[s, n], fict)
        f_out[at, :] = fict
        return 0

    lax.fori_loop(0, PIECES, piece, 0)
    own = jnp.concatenate([beside_each_other(lambda n: heat[s, n], 32) for s in range(PIECES)], axis=0)
    mine[...] = turned(own)
    side[...] = turned(jnp.concatenate([heat[s, TICKS] for s in range(PIECES)], axis=0))


def ready(heat, fictive):
    full = pl.BlockSpec(memory_space=VMEM)
    factor = jax.ShapeDtypeStruct((TICKS, EXT + PAD, COLS), F32)
    row_t = jax.ShapeDtypeStruct((COLS, ROWS), F32)
    return pl.pallas_call(
        ready_body,
        out_shape=[factor, factor, jax.ShapeDtypeStruct((ROWS, COLS), F32), row_t, row_t],
        in_specs=[full] * 2,
        out_specs=[full] * 5,
        compiler_params=params(16),
        cost_estimate=work(6),
        name="ready",
    )(heat, fictive)


def lay_body(flags, first, first_halo, got, got_dense, z, v, fict, got_halo):
    rest = SUBS - 2 * DEEP
    lane = iota((416, COLS), 1)
    blank = jnp.where((iota((416, COLS), 0) >= 380) & (iota((416, COLS), 0) < 390), 1.0, 0.0)
    got_halo[...] = jnp.where((lane < HALO) | (lane >= COLS - HALO), spread(got_dense[...]), blank)
    for lanes, own, left in ((slice(0, ROWS), first, got), (slice(ROWS, LANES), first_halo, got_halo)):
        width = lanes.stop - lanes.start
        for k in range(36):
            z[k, 0:DEEP, lanes] = left[DEEP * k:DEEP * k + DEEP, :]
            z[k, DEEP:2 * DEEP, lanes] = own[DEEP * k:DEEP * k + DEEP, :]
            z[k, 2 * DEEP:SUBS, lanes] = jnp.zeros((rest, width), F32)
        for k in range(2):
            v[k, 0:DEEP, lanes] = left[360 + DEEP * k:370 + DEEP * k, :]
            v[k, DEEP:SUBS, lanes] = own[360 + 16 * k:360 + 16 * k + SUBS - DEEP, :]
        fict[0:DEEP, lanes] = jnp.where(flags[2] == 1, OUTSIDE, left[380:390, :])
        fict[DEEP:2 * DEEP, lanes] = own[392:402, :]
        fict[2 * DEEP:SUBS, lanes] = jnp.ones((rest, width), F32)


def lay(flags, first, first_halo, got, got_halo):
    full = pl.BlockSpec(memory_space=VMEM)
    shapes = [(36, SUBS, LANES), (2, SUBS, LANES), (SUBS, LANES)]
    return pl.pallas_call(
        lay_body,
        out_shape=[jax.ShapeDtypeStruct(s, F32) for s in shapes],
        in_specs=[pl.BlockSpec(memory_space=SMEM)] + [full] * 4,
        out_specs=[full] * 3,
        scratch_shapes=[VMEM((416, COLS), F32)],
        compiler_params=params(8),
        cost_estimate=work(2),
        name="lay",
    )(flags, first, first_halo, got, got_halo)


def strip_body(flags, coef, z_in, v_in, fict_in, mine, side, heat_up, heat_down, nodes, z, v, q, heat_t):
    rest = SUBS - 2 * DEEP
    v[...] = v_in[...]
    q[...] = jnp.zeros((3, SUBS, LANES), F32)

    top, bottom = flags[0] == 1, flags[1] == 1
    last_side = corner(jnp.where(top, OUTSIDE, heat_up[TICKS]), jnp.where(bottom, OUTSIDE, heat_down[TICKS]), 1.0)
    last_mine = corner(beside_each_other(lambda n: jnp.where(top, OUTSIDE, heat_up[n]), HALO),
                       beside_each_other(lambda n: jnp.where(bottom, OUTSIDE, heat_down[n]), HALO), 1.0)
    for n in range(TICKS):
        cols = slice(DEEP * n, DEEP * n + DEEP)
        heat_t[n, 0:DEEP, 0:ROWS] = side[cols, :]
        heat_t[n, 0:DEEP, ROWS:LANES] = last_side[cols]
        heat_t[n, DEEP:2 * DEEP, 0:ROWS] = mine[cols, :]
        heat_t[n, DEEP:2 * DEEP, ROWS:LANES] = last_mine[cols]
        heat_t[n, 2 * DEEP:SUBS, :] = jnp.ones((rest, LANES), F32)

    lane = iota((SUBS, LANES), 1)
    inside = jnp.where(bottom & (lane >= ROWS) & (lane < LANES - HALO), 0.0, 1.0)
    sum_a = coef[24]
    nodes[...] = jnp.zeros((32, LANES), F32)
    nodes[31:32, :] = v[0, DEEP:DEEP + 1, :]
    nodes[0:1, :] = v[1, DEEP:DEEP + 1, :]

    def tick(n, fict):
        inv, half, fict_next = advance(heat_t[n], fict)

        def grads(m):
            beside = pltpu.roll(m, SUBS - 1, 0)
            both, diff = m + beside, beside - m
            return pltpu.roll(both, LANES - 1, 1) - both, pltpu.roll(diff, LANES - 1, 1) + diff

        u, w = v[0], v[1]
        lu, wu = grads(u)
        lw, ww = grads(w)
        now = [half * lu, half * ww, (0.5 * half) * (wu + lw)]
        delta = [q[c] - now[c] for c in range(3)]
        for c in range(3):
            q[c] = now[c]
        total = [sum_a * now[c] for c in range(3)]
        for k in range(MODES):
            kept = jnp.exp2(inv * coef[k])
            a = coef[12 + k]
            for c in range(3):
                new = kept * (z[3 * k + c] + a * delta[c])
                z[3 * k + c] = new
                total[c] = total[c] + new

        def force(lin, cross):
            a, b = lin + cross, lin - cross
            return 0.5 * ((a - pltpu.roll(b, 1, 1)) + pltpu.roll(b - pltpu.roll(a, 1, 1), 1, 0))

        u_next = (u + force(total[0], total[2])) * inside
        w_next = (w + force(total[2], total[1])) * inside
        v[0], v[1] = u_next, w_next
        nodes[pl.ds(2 * n + 1, 1), :] = u_next[DEEP:DEEP + 1]
        nodes[pl.ds(2 * n + 2, 1), :] = w_next[DEEP:DEEP + 1]
        return fict_next

    lax.fori_loop(0, TICKS, tick, fict_in[...])


def strip(flags, coef, z, v, fict, mine, side, heat_up, heat_down):
    full = pl.BlockSpec(memory_space=VMEM)
    smem = pl.BlockSpec(memory_space=SMEM)
    return pl.pallas_call(
        strip_body,
        out_shape=[jax.ShapeDtypeStruct((32, LANES), F32), jax.ShapeDtypeStruct((36, SUBS, LANES), F32)],
        in_specs=[smem, smem] + [full] * 7,
        out_specs=[full, full],
        input_output_aliases={2: 1},
        scratch_shapes=[
            VMEM((2, SUBS, LANES), F32),
            VMEM((3, SUBS, LANES), F32),
            VMEM((TICKS, SUBS, LANES), F32),
        ],
        compiler_params=params(16),
        cost_estimate=work(7),
        name="strip",
    )(flags, coef, z, v, fict, mine, side, heat_up, heat_down)[0]


def upright(nodes, i):
    part = nodes[:, i * COLS:(i + 1) * COLS]
    return jnp.concatenate([part[:24], jnp.zeros((COLS - 32, COLS), F32), part[24:]], axis=0).T


def edges_body(flags, inv_in, half_in, up, down, heat_up, heat_down, nodes, inv_ref, half_ref, left):
    top, bottom = flags[0] == 1, flags[1] == 1
    fict = jnp.concatenate([jnp.where(top, OUTSIDE, up[38]), jnp.where(bottom, OUTSIDE, down[38])], axis=0)
    for n in range(TICKS):
        theta = jnp.concatenate([jnp.where(top, OUTSIDE, heat_up[n]), jnp.where(bottom, OUTSIDE, heat_down[n])], axis=0)
        inv, half, fict = advance(theta, fict)
        inv_ref[n, 0:HALO, :] = inv[:HALO]
        half_ref[n, 0:HALO, :] = half[:HALO]
        inv_ref[n, HALO + ROWS:EXT, :] = inv[HALO:]
        half_ref[n, HALO + ROWS:EXT, :] = half[HALO:]
        inv_ref[n, EXT:EXT + PAD, :] = jnp.ones((PAD, COLS), F32)
        half_ref[n, EXT:EXT + PAD, :] = jnp.ones((PAD, COLS), F32)
    for i in range(5):
        part = upright(nodes, i)
        for n in range(TICKS):
            for c in range(2):
                moved = pltpu.roll(part, COLS - (2 * n + 1 + c), 1)
                if i < 4:
                    left[n, c, HALO + i * COLS:HALO + (i + 1) * COLS, :] = moved
                else:
                    left[n, c, HALO + ROWS:EXT, :] = moved[:HALO]
                    left[n, c, 0:HALO, :] = moved[COLS - HALO:]


def edges(flags, inv, half, up, down, heat_up, heat_down, nodes):
    full = pl.BlockSpec(memory_space=VMEM)
    factor = jax.ShapeDtypeStruct((TICKS, EXT + PAD, COLS), F32)
    return pl.pallas_call(
        edges_body,
        out_shape=[factor, factor, jax.ShapeDtypeStruct((TICKS, 2, EXT, COLS), F32)],
        in_specs=[pl.BlockSpec(memory_space=SMEM)] + [full] * 7,
        out_specs=[full] * 3,
        input_output_aliases={1: 0, 2: 1},
        compiler_params=params(18),
        cost_estimate=work(3),
        name="edges",
    )(flags, inv, half, up, down, heat_up, heat_down, nodes)


def block_body(flags, coef, state, motion, up, down, inv_ref, half_ref, left, beside_t, v_out, s_out, z, v, q, h, pairs, forces, zh, sem, in_sem):
    bottom = flags[1] == 1

    def in_copy(b):
        at = pl.ds(32 * b if isinstance(b, int) else pl.multiple_of(32 * b, 32), 32)
        return pltpu.make_async_copy(state.at[:, at], z.at[:, at], in_sem.at[b])

    for b in range(ROWS // 32):
        in_copy(b).start()

    for k in range(36):
        zh[k, 0:HALO, :] = up[k]
        zh[k, HALO:, :] = down[k]
    for c in range(2):
        v[c, 0:HALO, :] = up[36 + c]
        v[c, HALO:HALO + ROWS, :] = motion[c]
        v[c, HALO + ROWS:EXT, :] = down[36 + c]
        v[c, EXT:, :] = jnp.zeros((32, COLS), F32)
    q[...] = jnp.zeros((3, EXT + PAD, COLS), F32)
    forces[:, 0:8, :] = jnp.zeros((4, 8, COLS), F32)
    for i in range(5):
        part = upright(beside_t, i)
        if i < 4:
            h[HALO + i * COLS:HALO + (i + 1) * COLS, :] = part
        else:
            h[HALO + ROWS:EXT, :] = part[0:HALO]
            h[0:HALO, :] = part[COLS - HALO:]
            h[EXT:, :] = jnp.zeros((32, COLS), F32)

    lane = iota((FLOW, COLS), 1)
    at_right, at_left = lane == COLS - 1, lane == 0
    sum_a = coef[24]

    def out_copy(b):
        at = pl.ds(pl.multiple_of(32 * (b - 1), 32), 32)
        return pltpu.make_async_copy(z.at[:, at], s_out.at[:, at], sem.at[b - 1])

    def flow(n, forced, paired):
        for r in range(0, EXT, FLOW):
            at, here, above = pl.ds(r, FLOW), pl.ds(r + 8, FLOW), pl.ds(r + 7, FLOW)
            m = [v[c, at, :] for c in range(2)]
            if forced:
                for c in range(2):
                    lin, cross = 2 * c, 2 * c + 1
                    straight = forces[lin, here, :] - forces[cross, above, :]
                    turned_in = pltpu.roll(forces[cross, here, :] - forces[lin, above, :], 1, 1)
                    m[c] = jnp.where(at_left, left[n, c, at, :], m[c] + 0.5 * (straight + turned_in))
                    if r + FLOW == EXT:
                        m[c] = jnp.concatenate([m[c][:FLOW - HALO], jnp.where(bottom, 0.0, m[c][FLOW - HALO:])], axis=0)
                    v[c, at, :] = m[c]
            if paired:
                hist = h[at, :]
                h[at, :] = pltpu.roll(hist, COLS - 2, 1)
                beside = (jnp.where(at_right, hist, pltpu.roll(m[0], COLS - 1, 1)),
                          pltpu.roll(jnp.where(at_left, hist, m[1]), COLS - 1, 1))
                for c in range(2):
                    pairs[2 * c, at, :] = m[c] + beside[c]
                    pairs[2 * c + 1, at, :] = beside[c] - m[c]

    def relax(n, r, zs, r_z, size, final):
        at, below, at_z = pl.ds(r, size), pl.ds(r + 1, size), pl.ds(r_z, size)
        along = [pairs[2 * c, below, :] - pairs[2 * c, at, :] for c in range(2)]
        across = [pairs[2 * c + 1, below, :] + pairs[2 * c + 1, at, :] for c in range(2)]
        half, inv = half_ref[n, at, :], inv_ref[n, at, :]
        now = [half * along[0], half * across[1], (0.5 * half) * (across[0] + along[1])]
        delta = [q[c, at, :] - now[c] for c in range(3)]
        for c in range(3):
            q[c, at, :] = now[c]
        total = [sum_a * x for x in now]
        for k in range(MODES):
            kept = jnp.exp2(inv * coef[k])
            a = coef[12 + k]
            for c in range(3):
                new = kept * (zs[3 * k + c, at_z, :] + a * delta[c])
                zs[3 * k + c, at_z, :] = (new + a * now[c]) if final else new
                total[c] = total[c] + new
        xx, yy, xy = total
        for i, part in enumerate((xx + xy, xx - xy, xy + yy, xy - yy)):
            forces[i, pl.ds(r + 8, size), :] = part

    def relax_group(n, b, final):
        fixed = isinstance(b, int)
        size = HALO if fixed else SUB
        for t in range(0, 32, size):
            r = 32 * b + t
            if not fixed:
                r = pl.multiple_of(r, 8)
            if fixed and b == 0 and t < HALO:
                relax(n, r, zh, t, size, final)
            elif fixed and b > 0 and t >= HALO:
                relax(n, r, zh, t, size, final)
            else:
                relax(n, r, z, r - HALO, size, final)

    def tick(n, starting, final):
        if starting:
            in_copy(0).wait()
        relax_group(n, 0, final)

        def body(b, _):
            if starting:
                in_copy(b).wait()
            relax_group(n, b, final)
            if final:
                out_copy(b).start()
            return 0

        last = EXT // 32 - 1
        lax.fori_loop(1, last, body, 0)
        relax_group(n, last, final)
        if final:
            out_copy(last).start()
        flow(n, True, not final)

    def step(n, _):
        tick(n, False, False)
        return 0

    flow(0, False, True)
    tick(0, True, False)
    lax.fori_loop(1, TICKS - 1, step, 0)
    tick(TICKS - 1, False, True)
    for c in range(2):
        v_out[c] = v[c, HALO:HALO + ROWS, :]
    for b in range(1, EXT // 32):
        out_copy(b).wait()


def block(flags, coef, state, motion, up, down, inv, half, left, beside):
    full = pl.BlockSpec(memory_space=VMEM)
    smem = pl.BlockSpec(memory_space=SMEM)
    return pl.pallas_call(
        block_body,
        out_shape=[
            jax.ShapeDtypeStruct((2, ROWS, COLS), F32),
            pltpu.HBM((36, ROWS, COLS), F32),
        ],
        in_specs=[smem, smem, pl.BlockSpec(memory_space=pltpu.HBM)] + [full] * 7,
        out_specs=[full, pl.BlockSpec(memory_space=pltpu.HBM)],
        scratch_shapes=[
            VMEM((36, ROWS, COLS), F32),
            VMEM((2, EXT + 32, COLS), F32),
            VMEM((3, EXT + PAD, COLS), F32),
            VMEM((EXT + 32, COLS), F32),
            VMEM((4, EXT + 32, COLS), F32),
            VMEM((4, EXT + 8, COLS), F32),
            VMEM((36, 2 * HALO, COLS), F32),
            pltpu.SemaphoreType.DMA((EXT // 32 - 1,)),
            pltpu.SemaphoreType.DMA((ROWS // 32,)),
        ],
        compiler_params=params(26),
        cost_estimate=work(28),
        name="block",
    )(flags, coef, pinned(state), motion, up, down, inv, half, left, beside)


def shards(warmth_history, fictitious_warmth, vertex_velocity, branch_load_tensors, mechanism_lifetimes, branch_stiffness):
    state = branch_load_tensors.reshape(3 * MODES, ROWS, COLS)
    weight = 2.0 * branch_stiffness * mechanism_lifetimes
    coef = jnp.concatenate([-LOG2E / mechanism_lifetimes, weight, jnp.sum(weight)[None]])
    draw, wide = lax.axis_index("draw"), lax.axis_index(WIDE)
    flags = jnp.stack([draw == 0, draw == lax.axis_size("draw") - 1, wide == 0]).astype(jnp.int32)

    slab, above, below = cut(warmth_history, state, vertex_velocity, fictitious_warmth)
    heat = lax.all_to_all(slab, WIDE, split_axis=0, concat_axis=0, tiled=True)
    up = shifted(above, "draw", 1)
    down = shifted(below, "draw", -1)
    first, final = pack_own(state, vertex_velocity, fictitious_warmth)
    got = shifted(final, WIDE, 1)
    first_halo, final_halo = pack_halo(flags, up, down)
    got_halo = shifted(final_halo, WIDE, 1)
    heat_up = shifted(heat[PIECES - 1, :, HALO:, :], "draw", 1)
    heat_down = shifted(heat[0, :, :HALO, :], "draw", -1)
    inv, half, fict, mine, side = ready(heat, fictitious_warmth)
    got, got_halo, mine = lax.optimization_barrier((got, got_halo, mine))
    strip_state = lay(flags, first, first_halo, got, got_halo)
    nodes = strip(flags, coef, *strip_state, mine, side, heat_up, heat_down)
    beside = shifted(nodes, WIDE, -1)
    inv, half, left = edges(flags, inv, half, up, down, heat_up, heat_down, nodes)
    motion, modes = block(flags, coef, state, vertex_velocity, up, down, inv, half, left, beside)
    return fict, motion, modes.reshape(branch_load_tensors.shape)


def solution(mesh):
    in_specs = (
        P(None, ("draw", "width", "cores"), None),
        P("draw", ("width", "cores")),
        P(None, "draw", ("width", "cores")),
        P(None, None, "draw", ("width", "cores")),
        P(),
        P(),
    )
    out_specs = (
        P("draw", ("width", "cores")),
        P(None, "draw", ("width", "cores")),
        P(None, None, "draw", ("width", "cores")),
    )
    return jax.shard_map(shards, mesh=mesh, in_specs=in_specs, out_specs=out_specs, check_vma=False)
```

```python
import jax
import jax.numpy as jnp
from jax import lax
from jax.experimental import pallas as pl
from jax.experimental.pallas import tpu as pltpu
from jax.sharding import PartitionSpec as P

LOG2E = 1.4426950408889634
OUTSIDE = -1.0 / 3.0
TICKS = 10
MODES = 12
PIECES = 16
ROWS = 512
COLS = 128
HALO = 16
EXT = ROWS + 2 * HALO
DEEP = 10
LANES = 640
SUBS = 24
PAD = 8
EDGE = 392
SPAN = 3
SUB = 16
FLOW = 272
F32 = jnp.float32
VMEM = pltpu.VMEM
ANY = pl.ANY
SMEM = pltpu.SMEM
WIDE = ("width", "cores")


def shifted(shard, axis, by):
    peers = lax.axis_size(axis)
    pairs = [(i, i + by) for i in range(peers) if 0 <= i + by < peers]
    return lax.ppermute(shard, axis, pairs)


def params(mb):
    return pltpu.CompilerParams(vmem_limit_bytes=mb << 20)


def iota(shape, axis):
    return lax.broadcasted_iota(jnp.int32, shape, axis)


def pinned(x):
    return pltpu.with_memory_space_constraint(x, pltpu.HBM)


def cut_body(src, state, motion, fictive, dst, above, below, buf, side, halo, in_sem, out_sem, side_sem, row_sem):
    def fetch(p):
        return pltpu.make_async_copy(src.at[:, :, pl.ds(p * COLS, COLS)], buf.at[p], in_sem.at[p])

    def put(p):
        return pltpu.make_async_copy(buf.at[p], dst.at[p, pl.ds(0, TICKS)], out_sem.at[p])

    def put_side(p):
        return pltpu.make_async_copy(side.at[p], dst.at[p, TICKS], side_sem.at[p])

    ins, outs = [], []
    for i, (to, at) in enumerate(((above, ROWS - HALO), (below, 0))):
        part = pl.ds(at, HALO)
        for x, y in ((state.at[:, part], pl.ds(0, 36)), (motion.at[:, part], pl.ds(36, 2)), (fictive.at[part], 38)):
            ins.append(pltpu.make_async_copy(x, halo.at[i, y], row_sem.at[len(ins)]))
        outs.append(pltpu.make_async_copy(halo.at[i], to, row_sem.at[6 + i]))
    for p in range(PIECES):
        fetch(p).start()
    for c in ins:
        c.start()
    lane = iota((32, COLS), 1)
    for p in range(PIECES):
        fetch(p).wait()
        put(p).start()
        if p == 0:
            side[0] = jnp.full((32, COLS), OUTSIDE, F32)
            put_side(0).start()
        if p + 1 < PIECES:
            acc = jnp.full((32, COLS), 1.0, F32)
            for n in range(TICKS):
                moved = pltpu.roll(buf[p, n], (DEEP * n + DEEP) % COLS, 1)
                acc = jnp.where((lane >= DEEP * n) & (lane < DEEP * n + DEEP), moved, acc)
            side[p + 1] = acc
            put_side(p + 1).start()
    for c in ins:
        c.wait()
    for c in outs:
        c.start()
    for p in range(PIECES):
        put(p).wait()
        put_side(p).wait()
    for c in outs:
        c.wait()


def cut(slab, state, motion, fictive):
    hbm = pl.BlockSpec(memory_space=pltpu.HBM)
    halo = pltpu.HBM((39, HALO, COLS), F32)
    return pl.pallas_call(
        cut_body,
        out_shape=[pltpu.HBM((PIECES, TICKS + 1, 32, COLS), F32), halo, halo],
        in_specs=[hbm] * 4,
        out_specs=[hbm] * 3,
        scratch_shapes=[
            VMEM((PIECES, TICKS, 32, COLS), F32),
            VMEM((PIECES, 32, COLS), F32),
            VMEM((2, 39, HALO, COLS), F32),
            pltpu.SemaphoreType.DMA((PIECES,)),
            pltpu.SemaphoreType.DMA((PIECES,)),
            pltpu.SemaphoreType.DMA((PIECES,)),
            pltpu.SemaphoreType.DMA((8,)),
        ],
        compiler_params=params(8),
        name="cut",
    )(pinned(slab), pinned(state), pinned(motion), pinned(fictive))


def corner(up, down, fill):
    return jnp.concatenate([down, jnp.full((COLS - 2 * HALO, COLS), fill, F32), up], axis=0).T


def turned(own):
    return jnp.concatenate([own[i * COLS:(i + 1) * COLS].T for i in range(4)], axis=1)


def pack_body(flags, state, motion, fictive, up, down, first_out, send, buf, tail, first, more, sem, more_sem):
    copies = [pltpu.make_async_copy(state.at[pl.ds(4 * i, 4)], buf.at[pl.ds(4 * i, 4)], sem.at[i]) for i in range(9)]
    rest = [pltpu.make_async_copy(motion, more.at[pl.ds(0, 2)], more_sem.at[0]), pltpu.make_async_copy(fictive, more.at[2], more_sem.at[1])]
    for c in rest + copies:
        c.start()

    def put(at, blocks, corners, widths):
        for i in range(5):
            parts = corners if i == 4 else [b[i * COLS:(i + 1) * COLS].T for b in blocks]
            lanes = slice(i * COLS, (i + 1) * COLS)
            own = jnp.concatenate([p[:w] for p, w in zip(parts, widths)], axis=0)
            first[at:at + own.shape[0], lanes] = own
            gone = [p[COLS - DEEP:] for p in parts]
            if len(gone) == 3:
                gone.append(jnp.zeros((2, COLS), F32))
            gone = jnp.concatenate(gone, axis=0)
            if i < 4:
                send[EDGE * i + at:EDGE * i + at + gone.shape[0], :] = gone
            else:
                tail[at:at + gone.shape[0], :] = gone

    f_up = jnp.where(flags[0] == 1, OUTSIDE, up[38])
    f_down = jnp.where(flags[1] == 1, OUTSIDE, down[38])
    for c in rest:
        c.wait()
    put(360, [more[0], more[1], more[2]], [corner(up[36], down[36], 0.0), corner(up[37], down[37], 0.0), corner(f_up, f_down, 1.0)], (16, 16, 16))
    for i in range(9):
        copies[i].wait()
        put(40 * i, [buf[4 * i + j] for j in range(4)], [corner(up[4 * i + j], down[4 * i + j], 0.0) for j in range(4)], (DEEP,) * 4)
    keep = pltpu.make_async_copy(first, first_out, more_sem.at[2])
    keep.start()
    tail[EDGE:416, :] = jnp.zeros((416 - EDGE, COLS), F32)
    lane = iota((104, COLS), 1)
    acc = jnp.zeros((104, COLS), F32)
    for j in range(4):
        moved = pltpu.roll(tail[104 * j:104 * j + 104, :], (HALO + 32 * j) % COLS, 1)
        acc = jnp.where((lane >= 32 * j) & (lane < 32 * j + 32), moved, acc)
    send[4 * EDGE:, :] = acc
    keep.wait()


def spread(dense):
    return jnp.concatenate([pltpu.roll(dense, COLS - HALO - 32 * j, 1) for j in range(4)], axis=0)


def pack(flags, state, motion, fictive, up, down):
    full = pl.BlockSpec(memory_space=VMEM)
    hbm = pl.BlockSpec(memory_space=pltpu.HBM)
    return pl.pallas_call(
        pack_body,
        out_shape=[pltpu.HBM((408, LANES), F32), jax.ShapeDtypeStruct((4 * EDGE + 104, COLS), F32)],
        in_specs=[pl.BlockSpec(memory_space=SMEM)] + [hbm] * 3 + [full] * 2,
        out_specs=[hbm, full],
        scratch_shapes=[
            VMEM((36, ROWS, COLS), F32),
            VMEM((416, COLS), F32),
            VMEM((408, LANES), F32),
            VMEM((3, ROWS, COLS), F32),
            pltpu.SemaphoreType.DMA((9,)),
            pltpu.SemaphoreType.DMA((3,)),
        ],
        compiler_params=params(20),
        name="pack",
    )(flags, pinned(state), pinned(motion), pinned(fictive), up, down)


def shift_of(theta, fict):
    arg = 10.0 * (theta + fict) / (theta * fict) - 20.0
    inv = jnp.exp(-arg)
    return inv, jnp.exp(arg)


def work(us):
    return pl.CostEstimate(flops=0, transcendentals=0, bytes_accessed=us * 3_000_000)


def beside_each_other(pick, rows):
    lane = iota((rows, COLS), 1)
    acc = jnp.full((rows, COLS), 1.0, F32)
    for n in range(TICKS):
        moved = pltpu.roll(pick(n), DEEP * n, 1) if n else pick(n)
        acc = jnp.where((lane >= DEEP * n) & (lane < DEEP * n + DEEP), moved, acc)
    return acc


def advance(theta, fict):
    inv, shift = shift_of(theta, fict)
    return inv, 0.5 * shift, theta + (fict - theta) * jnp.exp(inv * (-1.0 / 3.0))


def ready_body(heat, mine, side):
    own = jnp.concatenate([beside_each_other(lambda n: heat[s, n], 32) for s in range(PIECES)], axis=0)
    mine[...] = turned(own)
    side[...] = turned(jnp.concatenate([heat[s, TICKS] for s in range(PIECES)], axis=0))


def ready(heat):
    full = pl.BlockSpec(memory_space=VMEM)
    row_t = jax.ShapeDtypeStruct((COLS, ROWS), F32)
    return pl.pallas_call(
        ready_body,
        out_shape=[row_t, row_t],
        in_specs=[full],
        out_specs=[full] * 2,
        compiler_params=params(8),
        cost_estimate=work(3),
        name="ready",
    )(heat)


def lay_body(flags, first, got, z, v, fict, got_halo):
    rest = SUBS - 2 * DEEP
    lane = iota((416, COLS), 1)
    blank = jnp.where((iota((416, COLS), 0) >= 380) & (iota((416, COLS), 0) < 390), 1.0, 0.0)
    got_halo[...] = jnp.where((lane < HALO) | (lane >= COLS - HALO), spread(got[4 * EDGE:, :]), blank)
    for k in range(36):
        z[k, DEEP:2 * DEEP, :] = first[DEEP * k:DEEP * k + DEEP, :]
        z[k, 2 * DEEP:SUBS, :] = jnp.zeros((rest, LANES), F32)
    for k in range(2):
        v[k, DEEP:SUBS, :] = first[360 + 16 * k:360 + 16 * k + SUBS - DEEP, :]
    fict[DEEP:2 * DEEP, :] = first[392:402, :]
    fict[2 * DEEP:SUBS, :] = jnp.ones((rest, LANES), F32)
    for i in range(5):
        lanes = slice(i * COLS, (i + 1) * COLS)
        left = got_halo if i == 4 else got.at[pl.ds(EDGE * i, EDGE)]
        for k in range(36):
            z[k, 0:DEEP, lanes] = left[DEEP * k:DEEP * k + DEEP, :]
        for k in range(2):
            v[k, 0:DEEP, lanes] = left[360 + DEEP * k:370 + DEEP * k, :]
        fict[0:DEEP, lanes] = jnp.where(flags[2] == 1, OUTSIDE, left[380:390, :])


def lay(flags, first, got):
    full = pl.BlockSpec(memory_space=VMEM)
    shapes = [(36, SUBS, LANES), (2, SUBS, LANES), (SUBS, LANES)]
    return pl.pallas_call(
        lay_body,
        out_shape=[jax.ShapeDtypeStruct(s, F32) for s in shapes],
        in_specs=[pl.BlockSpec(memory_space=SMEM)] + [full] * 2,
        out_specs=[full] * 3,
        scratch_shapes=[VMEM((416, COLS), F32)],
        compiler_params=params(8),
        cost_estimate=work(2),
        name="lay",
    )(flags, first, got)


def strip_body(flags, coef, z_in, v_in, fict_in, mine, side, heat_up, heat_down, nodes, z, v, q, heat_t):
    rest = SUBS - 2 * DEEP
    v[...] = v_in[...]
    q[...] = jnp.zeros((3, SUBS, LANES), F32)

    top, bottom = flags[0] == 1, flags[1] == 1
    last_side = corner(jnp.where(top, OUTSIDE, heat_up[TICKS]), jnp.where(bottom, OUTSIDE, heat_down[TICKS]), 1.0)
    last_mine = corner(beside_each_other(lambda n: jnp.where(top, OUTSIDE, heat_up[n]), HALO),
                       beside_each_other(lambda n: jnp.where(bottom, OUTSIDE, heat_down[n]), HALO), 1.0)
    for n in range(TICKS):
        cols = slice(DEEP * n, DEEP * n + DEEP)
        heat_t[n, 0:DEEP, 0:ROWS] = side[cols, :]
        heat_t[n, 0:DEEP, ROWS:LANES] = last_side[cols]
        heat_t[n, DEEP:2 * DEEP, 0:ROWS] = mine[cols, :]
        heat_t[n, DEEP:2 * DEEP, ROWS:LANES] = last_mine[cols]
        heat_t[n, 2 * DEEP:SUBS, :] = jnp.ones((rest, LANES), F32)

    inside = jnp.where(bottom & (iota((8, LANES), 1) >= ROWS) & (iota((8, LANES), 1) < LANES - HALO), 0.0, 1.0)
    sum_a = coef[24]
    nodes[...] = jnp.zeros((32, LANES), F32)
    nodes[31:32, :] = v[0, DEEP:DEEP + 1, :]
    nodes[0:1, :] = v[1, DEEP:DEEP + 1, :]

    def tick(n, fict, lo, hi):
        at, size = slice(lo, hi), hi - lo
        inv, half, fict_next = advance(heat_t[n, at], fict)
        keep = jnp.concatenate([inside] * (size // 8), axis=0)

        def grads(m):
            beside = pltpu.roll(m, size - 1, 0)
            both, diff = m + beside, beside - m
            return pltpu.roll(both, LANES - 1, 1) - both, pltpu.roll(diff, LANES - 1, 1) + diff

        u, w = v[0, at], v[1, at]
        lu, wu = grads(u)
        lw, ww = grads(w)
        now = [half * lu, half * ww, (0.5 * half) * (wu + lw)]
        delta = [q[c, at] - now[c] for c in range(3)]
        for c in range(3):
            q[c, at] = now[c]
        total = [sum_a * now[c] for c in range(3)]
        for k in range(MODES):
            kept = jnp.exp2(inv * coef[k])
            a = coef[12 + k]
            for c in range(3):
                new = kept * (z[3 * k + c, at] + a * delta[c])
                z[3 * k + c, at] = new
                total[c] = total[c] + new

        def force(lin, cross):
            a, b = lin + cross, lin - cross
            return 0.5 * ((a - pltpu.roll(b, 1, 1)) + pltpu.roll(b - pltpu.roll(a, 1, 1), 1, 0))

        u_next = (u + force(total[0], total[2])) * keep
        w_next = (w + force(total[2], total[1])) * keep
        v[0, at], v[1, at] = u_next, w_next
        nodes[pl.ds(2 * n + 1, 1), :] = u_next[DEEP - lo:DEEP - lo + 1]
        nodes[pl.ds(2 * n + 2, 1), :] = w_next[DEEP - lo:DEEP - lo + 1]
        return fict_next

    fict = lax.fori_loop(0, 5, lambda n, f: tick(n, f, 0, SUBS), fict_in[...])
    fict = lax.fori_loop(5, 8, lambda n, f: tick(n, f, 0, 16), fict[:16])
    lax.fori_loop(8, TICKS, lambda n, f: tick(n, f, 8, 16), fict[8:16])


def strip(flags, coef, z, v, fict, mine, side, heat_up, heat_down):
    full = pl.BlockSpec(memory_space=VMEM)
    smem = pl.BlockSpec(memory_space=SMEM)
    return pl.pallas_call(
        strip_body,
        out_shape=[jax.ShapeDtypeStruct((32, LANES), F32), jax.ShapeDtypeStruct((36, SUBS, LANES), F32)],
        in_specs=[smem, smem] + [full] * 7,
        out_specs=[full, full],
        input_output_aliases={2: 1},
        scratch_shapes=[
            VMEM((2, SUBS, LANES), F32),
            VMEM((3, SUBS, LANES), F32),
            VMEM((TICKS, SUBS, LANES), F32),
        ],
        compiler_params=params(16),
        cost_estimate=work(7),
        name="strip",
    )(flags, coef, z, v, fict, mine, side, heat_up, heat_down)[0]


def upright(nodes, i):
    part = nodes[:, i * COLS:(i + 1) * COLS]
    return jnp.concatenate([part[:24], jnp.zeros((COLS - 32, COLS), F32), part[24:]], axis=0).T


def edges_body(flags, heat, fictive, up, down, heat_up, heat_down, nodes, inv_ref, half_ref, f_out, left):
    for s in range(0, PIECES, 8):
        at, to = slice(32 * s, 32 * s + 256), slice(32 * s + HALO, 32 * s + HALO + 256)
        own = fictive[at, :]
        for n in range(TICKS):
            inv_ref[n, to, :], half_ref[n, to, :], own = advance(heat[s:s + 8, n].reshape(256, COLS), own)
        f_out[at, :] = own
    top, bottom = flags[0] == 1, flags[1] == 1
    fict = jnp.concatenate([jnp.where(top, OUTSIDE, up[38]), jnp.where(bottom, OUTSIDE, down[38])], axis=0)
    for n in range(TICKS):
        theta = jnp.concatenate([jnp.where(top, OUTSIDE, heat_up[n]), jnp.where(bottom, OUTSIDE, heat_down[n])], axis=0)
        inv, half, fict = advance(theta, fict)
        inv_ref[n, 0:HALO, :] = inv[:HALO]
        half_ref[n, 0:HALO, :] = half[:HALO]
        inv_ref[n, HALO + ROWS:EXT, :] = inv[HALO:]
        half_ref[n, HALO + ROWS:EXT, :] = half[HALO:]
        inv_ref[n, EXT:EXT + PAD, :] = jnp.ones((PAD, COLS), F32)
        half_ref[n, EXT:EXT + PAD, :] = jnp.ones((PAD, COLS), F32)
    for i in range(5):
        part = upright(nodes, i)
        for n in range(TICKS):
            for c in range(2):
                moved = pltpu.roll(part, COLS - (2 * n + 1 + c), 1)
                if i < 4:
                    left[n, c, HALO + i * COLS:HALO + (i + 1) * COLS, :] = moved
                else:
                    left[n, c, HALO + ROWS:EXT, :] = moved[:HALO]
                    left[n, c, 0:HALO, :] = moved[COLS - HALO:]


def edges(flags, heat, fictive, up, down, heat_up, heat_down, nodes):
    full = pl.BlockSpec(memory_space=VMEM)
    factor = jax.ShapeDtypeStruct((TICKS, EXT + PAD, COLS), F32)
    return pl.pallas_call(
        edges_body,
        out_shape=[factor, factor, jax.ShapeDtypeStruct((ROWS, COLS), F32), jax.ShapeDtypeStruct((TICKS, 2, EXT, COLS), F32)],
        in_specs=[pl.BlockSpec(memory_space=SMEM)] + [full] * 7,
        out_specs=[full] * 4,
        compiler_params=params(12),
        cost_estimate=work(6),
        name="edges",
    )(flags, heat, fictive, up, down, heat_up, heat_down, nodes)


def block_body(flags, coef, state, motion, up, down, inv_ref, half_ref, left, beside_t, v_out, s_out, z, v, q, h, pairs, forces, zh, sem, in_sem):
    bottom = flags[1] == 1

    def in_copy(b):
        at = pl.ds(32 * b if isinstance(b, int) else pl.multiple_of(32 * b, 32), 32)
        return pltpu.make_async_copy(state.at[:, at], z.at[:, at], in_sem.at[b])

    for b in range(ROWS // 32):
        in_copy(b).start()

    for k in range(36):
        zh[k, 0:HALO, :] = up[k]
        zh[k, HALO:, :] = down[k]
    for c in range(2):
        v[c, 0:HALO, :] = up[36 + c]
        v[c, HALO:HALO + ROWS, :] = motion[c]
        v[c, HALO + ROWS:EXT, :] = down[36 + c]
        v[c, EXT:, :] = jnp.zeros((32, COLS), F32)
    q[...] = jnp.zeros((3, EXT + PAD, COLS), F32)
    forces[:, 0:8, :] = jnp.zeros((4, 8, COLS), F32)
    for i in range(5):
        part = upright(beside_t, i)
        if i < 4:
            h[HALO + i * COLS:HALO + (i + 1) * COLS, :] = part
        else:
            h[HALO + ROWS:EXT, :] = part[0:HALO]
            h[0:HALO, :] = part[COLS - HALO:]
            h[EXT:, :] = jnp.zeros((32, COLS), F32)

    lane = iota((FLOW, COLS), 1)
    at_right, at_left = lane == COLS - 1, lane == 0
    sum_a = coef[24]

    def out_copy(b):
        at = pl.ds(pl.multiple_of(32 * (b - 1), 32), 32)
        return pltpu.make_async_copy(z.at[:, at], s_out.at[:, at], sem.at[b - 1])

    def flow(n, forced, paired):
        for r in range(0, EXT, FLOW):
            at, here, above = pl.ds(r, FLOW), pl.ds(r + 8, FLOW), pl.ds(r + 7, FLOW)
            m = [v[c, at, :] for c in range(2)]
            if forced:
                for c in range(2):
                    lin, cross = 2 * c, 2 * c + 1
                    straight = forces[lin, here, :] - forces[cross, above, :]
                    turned_in = pltpu.roll(forces[cross, here, :] - forces[lin, above, :], 1, 1)
                    m[c] = jnp.where(at_left, left[n, c, at, :], m[c] + 0.5 * (straight + turned_in))
                    if r + FLOW == EXT:
                        m[c] = jnp.concatenate([m[c][:FLOW - HALO], jnp.where(bottom, 0.0, m[c][FLOW - HALO:])], axis=0)
                    v[c, at, :] = m[c]
            if paired:
                hist = h[at, :]
                h[at, :] = pltpu.roll(hist, COLS - 2, 1)
                beside = (jnp.where(at_right, hist, pltpu.roll(m[0], COLS - 1, 1)),
                          pltpu.roll(jnp.where(at_left, hist, m[1]), COLS - 1, 1))
                for c in range(2):
                    pairs[2 * c, at, :] = m[c] + beside[c]
                    pairs[2 * c + 1, at, :] = beside[c] - m[c]

    def relax(n, r, zs, r_z, size, final):
        at, below, at_z = pl.ds(r, size), pl.ds(r + 1, size), pl.ds(r_z, size)
        along = [pairs[2 * c, below, :] - pairs[2 * c, at, :] for c in range(2)]
        across = [pairs[2 * c + 1, below, :] + pairs[2 * c + 1, at, :] for c in range(2)]
        half, inv = half_ref[n, at, :], inv_ref[n, at, :]
        now = [half * along[0], half * across[1], (0.5 * half) * (across[0] + along[1])]
        delta = [q[c, at, :] - now[c] for c in range(3)]
        for c in range(3):
            q[c, at, :] = now[c]
        total = [sum_a * x for x in now]
        for k in range(MODES):
            kept = jnp.exp2(inv * coef[k])
            a = coef[12 + k]
            for c in range(3):
                new = kept * (zs[3 * k + c, at_z, :] + a * delta[c])
                zs[3 * k + c, at_z, :] = (new + a * now[c]) if final else new
                total[c] = total[c] + new
        xx, yy, xy = total
        for i, part in enumerate((xx + xy, xx - xy, xy + yy, xy - yy)):
            forces[i, pl.ds(r + 8, size), :] = part

    def relax_group(n, b, final):
        fixed = isinstance(b, int)
        size = HALO if fixed else SUB
        for t in range(0, 32, size):
            r = 32 * b + t
            if not fixed:
                r = pl.multiple_of(r, 8)
            if fixed and b == 0 and t < HALO:
                relax(n, r, zh, t, size, final)
            elif fixed and b > 0 and t >= HALO:
                relax(n, r, zh, t, size, final)
            else:
                relax(n, r, z, r - HALO, size, final)

    def tick(n, starting, final):
        if starting:
            in_copy(0).wait()
        relax_group(n, 0, final)

        def body(i, _):
            for j in range(SPAN):
                b = SPAN * i + j + 1
                if starting:
                    in_copy(b).wait()
                relax_group(n, b, final)
                if final:
                    out_copy(b).start()
            return 0

        last = EXT // 32 - 1
        lax.fori_loop(0, (last - 1) // SPAN, body, 0)
        relax_group(n, last, final)
        if final:
            out_copy(last).start()
        flow(n, True, not final)

    def step(n, _):
        tick(n, False, False)
        return 0

    flow(0, False, True)
    tick(0, True, False)
    lax.fori_loop(1, TICKS - 1, step, 0)
    tick(TICKS - 1, False, True)
    for c in range(2):
        v_out[c] = v[c, HALO:HALO + ROWS, :]
    for b in range(1, EXT // 32):
        out_copy(b).wait()


def block(flags, coef, state, motion, up, down, inv, half, left, beside):
    full = pl.BlockSpec(memory_space=VMEM)
    smem = pl.BlockSpec(memory_space=SMEM)
    return pl.pallas_call(
        block_body,
        out_shape=[
            jax.ShapeDtypeStruct((2, ROWS, COLS), F32),
            pltpu.HBM((36, ROWS, COLS), F32),
        ],
        in_specs=[smem, smem, pl.BlockSpec(memory_space=pltpu.HBM)] + [full] * 7,
        out_specs=[full, pl.BlockSpec(memory_space=pltpu.HBM)],
        scratch_shapes=[
            VMEM((36, ROWS, COLS), F32),
            VMEM((2, EXT + 32, COLS), F32),
            VMEM((3, EXT + PAD, COLS), F32),
            VMEM((EXT + 32, COLS), F32),
            VMEM((4, EXT + 32, COLS), F32),
            VMEM((4, EXT + 8, COLS), F32),
            VMEM((36, 2 * HALO, COLS), F32),
            pltpu.SemaphoreType.DMA((EXT // 32 - 1,)),
            pltpu.SemaphoreType.DMA((ROWS // 32,)),
        ],
        compiler_params=params(26),
        cost_estimate=work(28),
        name="block",
    )(flags, coef, pinned(state), motion, up, down, inv, half, left, beside)


def shards(warmth_history, fictitious_warmth, vertex_velocity, branch_load_tensors, mechanism_lifetimes, branch_stiffness):
    state = branch_load_tensors.reshape(3 * MODES, ROWS, COLS)
    weight = 2.0 * branch_stiffness * mechanism_lifetimes
    coef = jnp.concatenate([-LOG2E / mechanism_lifetimes, weight, jnp.sum(weight)[None]])
    draw, wide = lax.axis_index("draw"), lax.axis_index(WIDE)
    flags = jnp.stack([draw == 0, draw == lax.axis_size("draw") - 1, wide == 0]).astype(jnp.int32)

    slab, above, below = cut(warmth_history, state, vertex_velocity, fictitious_warmth)
    heat = lax.all_to_all(slab, WIDE, split_axis=0, concat_axis=0, tiled=True)
    up = shifted(above, "draw", 1)
    down = shifted(below, "draw", -1)
    up, down, coef = lax.optimization_barrier((up, down, coef))
    first, final = pack(flags, state, vertex_velocity, fictitious_warmth, up, down)
    got = shifted(final, WIDE, 1)
    heat_up = shifted(heat[PIECES - 1, :, HALO:, :], "draw", 1)
    heat_down = shifted(heat[0, :, :HALO, :], "draw", -1)
    mine, side = ready(heat)
    got, mine = lax.optimization_barrier((got, mine))
    strip_state = lay(flags, first, got)
    nodes = strip(flags, coef, *strip_state, mine, side, heat_up, heat_down)
    beside = shifted(nodes, WIDE, -1)
    inv, half, fict, left = edges(flags, heat, fictitious_warmth, up, down, heat_up, heat_down, nodes)
    motion, modes = block(flags, coef, state, vertex_velocity, up, down, inv, half, left, beside)
    return fict, motion, modes.reshape(branch_load_tensors.shape)


def solution(mesh):
    in_specs = (
        P(None, ("draw", "width", "cores"), None),
        P("draw", ("width", "cores")),
        P(None, "draw", ("width", "cores")),
        P(None, None, "draw", ("width", "cores")),
        P(),
        P(),
    )
    out_specs = (
        P("draw", ("width", "cores")),
        P(None, "draw", ("width", "cores")),
        P(None, None, "draw", ("width", "cores")),
    )
    return jax.shard_map(shards, mesh=mesh, in_specs=in_specs, out_specs=out_specs, check_vma=False)
```

```python
import jax
import jax.numpy as jnp
from jax import lax
from jax.experimental import pallas as pl
from jax.experimental.pallas import tpu as pltpu
from jax.sharding import PartitionSpec as P

LOG2E = 1.4426950408889634
OUTSIDE = -1.0 / 3.0
TICKS = 10
MODES = 12
PIECES = 16
ROWS = 512
COLS = 128
HALO = 16
EXT = ROWS + 2 * HALO
DEEP = 10
LANES = 640
SUBS = 24
PAD = 8
EDGE = 392
SPAN = 3
SUB = 16
FLOW = 272
F32 = jnp.float32
VMEM = pltpu.VMEM
ANY = pl.ANY
SMEM = pltpu.SMEM
WIDE = ("width", "cores")


def shifted(shard, axis, by):
    peers = lax.axis_size(axis)
    pairs = [(i, i + by) for i in range(peers) if 0 <= i + by < peers]
    return lax.ppermute(shard, axis, pairs)


def params(mb):
    return pltpu.CompilerParams(vmem_limit_bytes=mb << 20)


def iota(shape, axis):
    return lax.broadcasted_iota(jnp.int32, shape, axis)


def pinned(x):
    return pltpu.with_memory_space_constraint(x, pltpu.HBM)


def cut_body(src, state, motion, fictive, dst, above, below, buf, side, halo, in_sem, out_sem, side_sem, row_sem):
    def fetch(p):
        return pltpu.make_async_copy(src.at[:, :, pl.ds(p * COLS, COLS)], buf.at[p], in_sem.at[p])

    def put(p):
        return pltpu.make_async_copy(buf.at[p], dst.at[p, pl.ds(0, TICKS)], out_sem.at[p])

    def put_side(p):
        return pltpu.make_async_copy(side.at[p], dst.at[p, TICKS], side_sem.at[p])

    ins, outs = [], []
    for i, (to, at) in enumerate(((above, ROWS - HALO), (below, 0))):
        part = pl.ds(at, HALO)
        for x, y in ((state.at[:, part], pl.ds(0, 36)), (motion.at[:, part], pl.ds(36, 2)), (fictive.at[part], 38)):
            ins.append(pltpu.make_async_copy(x, halo.at[i, y], row_sem.at[len(ins)]))
        outs.append(pltpu.make_async_copy(halo.at[i], to, row_sem.at[6 + i]))
    for p in range(PIECES):
        fetch(p).start()
    for c in ins:
        c.start()
    lane = iota((32, COLS), 1)
    for p in range(PIECES):
        fetch(p).wait()
        put(p).start()
        if p == 0:
            side[0] = jnp.full((32, COLS), OUTSIDE, F32)
            put_side(0).start()
        if p + 1 < PIECES:
            acc = jnp.full((32, COLS), 1.0, F32)
            for n in range(TICKS):
                moved = pltpu.roll(buf[p, n], (DEEP * n + DEEP) % COLS, 1)
                acc = jnp.where((lane >= DEEP * n) & (lane < DEEP * n + DEEP), moved, acc)
            side[p + 1] = acc
            put_side(p + 1).start()
    for c in ins:
        c.wait()
    for c in outs:
        c.start()
    for p in range(PIECES):
        put(p).wait()
        put_side(p).wait()
    for c in outs:
        c.wait()


def cut(slab, state, motion, fictive):
    hbm = pl.BlockSpec(memory_space=pltpu.HBM)
    halo = pltpu.HBM((39, HALO, COLS), F32)
    return pl.pallas_call(
        cut_body,
        out_shape=[pltpu.HBM((PIECES, TICKS + 1, 32, COLS), F32), halo, halo],
        in_specs=[hbm] * 4,
        out_specs=[hbm] * 3,
        scratch_shapes=[
            VMEM((PIECES, TICKS, 32, COLS), F32),
            VMEM((PIECES, 32, COLS), F32),
            VMEM((2, 39, HALO, COLS), F32),
            pltpu.SemaphoreType.DMA((PIECES,)),
            pltpu.SemaphoreType.DMA((PIECES,)),
            pltpu.SemaphoreType.DMA((PIECES,)),
            pltpu.SemaphoreType.DMA((8,)),
        ],
        compiler_params=params(8),
        name="cut",
    )(pinned(slab), pinned(state), pinned(motion), pinned(fictive))


def corner(up, down, fill):
    return jnp.concatenate([down, jnp.full((COLS - 2 * HALO, COLS), fill, F32), up], axis=0).T


def turned(own):
    return jnp.concatenate([own[i * COLS:(i + 1) * COLS].T for i in range(4)], axis=1)


def pack_body(flags, state, motion, fictive, up, down, first_out, send, buf, tail, first, more, sem, more_sem):
    copies = [pltpu.make_async_copy(state.at[pl.ds(4 * i, 4)], buf.at[pl.ds(4 * i, 4)], sem.at[i]) for i in range(9)]
    rest = [pltpu.make_async_copy(motion, more.at[pl.ds(0, 2)], more_sem.at[0]), pltpu.make_async_copy(fictive, more.at[2], more_sem.at[1])]
    for c in rest + copies:
        c.start()

    def put(at, blocks, corners, widths):
        for i in range(5):
            parts = corners if i == 4 else [b[i * COLS:(i + 1) * COLS].T for b in blocks]
            lanes = slice(i * COLS, (i + 1) * COLS)
            own = jnp.concatenate([p[:w] for p, w in zip(parts, widths)], axis=0)
            first[at:at + own.shape[0], lanes] = own
            gone = [p[COLS - DEEP:] for p in parts]
            if len(gone) == 3:
                gone.append(jnp.zeros((2, COLS), F32))
            gone = jnp.concatenate(gone, axis=0)
            if i < 4:
                send[EDGE * i + at:EDGE * i + at + gone.shape[0], :] = gone
            else:
                tail[at:at + gone.shape[0], :] = gone

    f_up = jnp.where(flags[0] == 1, OUTSIDE, up[38])
    f_down = jnp.where(flags[1] == 1, OUTSIDE, down[38])
    for c in rest:
        c.wait()
    put(360, [more[0], more[1], more[2]], [corner(up[36], down[36], 0.0), corner(up[37], down[37], 0.0), corner(f_up, f_down, 1.0)], (16, 16, 16))
    for i in range(9):
        copies[i].wait()
        put(40 * i, [buf[4 * i + j] for j in range(4)], [corner(up[4 * i + j], down[4 * i + j], 0.0) for j in range(4)], (DEEP,) * 4)
    keep = pltpu.make_async_copy(first, first_out, more_sem.at[2])
    keep.start()
    tail[EDGE:416, :] = jnp.zeros((416 - EDGE, COLS), F32)
    lane = iota((104, COLS), 1)
    acc = jnp.zeros((104, COLS), F32)
    for j in range(4):
        moved = pltpu.roll(tail[104 * j:104 * j + 104, :], (HALO + 32 * j) % COLS, 1)
        acc = jnp.where((lane >= 32 * j) & (lane < 32 * j + 32), moved, acc)
    send[4 * EDGE:, :] = acc
    keep.wait()


def spread(dense):
    return jnp.concatenate([pltpu.roll(dense, COLS - HALO - 32 * j, 1) for j in range(4)], axis=0)


def pack(flags, state, motion, fictive, up, down):
    full = pl.BlockSpec(memory_space=VMEM)
    hbm = pl.BlockSpec(memory_space=pltpu.HBM)
    return pl.pallas_call(
        pack_body,
        out_shape=[pltpu.HBM((408, LANES), F32), jax.ShapeDtypeStruct((4 * EDGE + 104, COLS), F32)],
        in_specs=[pl.BlockSpec(memory_space=SMEM)] + [hbm] * 3 + [full] * 2,
        out_specs=[hbm, full],
        scratch_shapes=[
            VMEM((36, ROWS, COLS), F32),
            VMEM((416, COLS), F32),
            VMEM((408, LANES), F32),
            VMEM((3, ROWS, COLS), F32),
            pltpu.SemaphoreType.DMA((9,)),
            pltpu.SemaphoreType.DMA((3,)),
        ],
        compiler_params=params(20),
        name="pack",
    )(flags, pinned(state), pinned(motion), pinned(fictive), up, down)


def shift_of(theta, fict):
    arg = 10.0 * (theta + fict) / (theta * fict) - 20.0
    inv = jnp.exp(-arg)
    return inv, jnp.exp(arg)


def work(us):
    return pl.CostEstimate(flops=0, transcendentals=0, bytes_accessed=us * 3_000_000)


def beside_each_other(pick, rows):
    lane = iota((rows, COLS), 1)
    acc = jnp.full((rows, COLS), 1.0, F32)
    for n in range(TICKS):
        moved = pltpu.roll(pick(n), DEEP * n, 1) if n else pick(n)
        acc = jnp.where((lane >= DEEP * n) & (lane < DEEP * n + DEEP), moved, acc)
    return acc


def advance(theta, fict):
    inv, shift = shift_of(theta, fict)
    return inv, 0.5 * shift, theta + (fict - theta) * jnp.exp(inv * (-1.0 / 3.0))


def ready_body(heat, mine, side):
    own = jnp.concatenate([beside_each_other(lambda n: heat[s, n], 32) for s in range(PIECES)], axis=0)
    mine[...] = turned(own)
    side[...] = turned(jnp.concatenate([heat[s, TICKS] for s in range(PIECES)], axis=0))


def ready(heat):
    full = pl.BlockSpec(memory_space=VMEM)
    row_t = jax.ShapeDtypeStruct((COLS, ROWS), F32)
    return pl.pallas_call(
        ready_body,
        out_shape=[row_t, row_t],
        in_specs=[full],
        out_specs=[full] * 2,
        compiler_params=params(8),
        cost_estimate=work(3),
        name="ready",
    )(heat)


def lay_body(flags, got, z_in, v_in, fict_in, z, v, fict, got_halo):
    lane = iota((416, COLS), 1)
    blank = jnp.where((iota((416, COLS), 0) >= 380) & (iota((416, COLS), 0) < 390), 1.0, 0.0)
    got_halo[...] = jnp.where((lane < HALO) | (lane >= COLS - HALO), spread(got[4 * EDGE:, :]), blank)
    for i in range(5):
        lanes = slice(i * COLS, (i + 1) * COLS)
        left = got_halo if i == 4 else got.at[pl.ds(EDGE * i, EDGE)]
        for k in range(36):
            z[k, 0:DEEP, lanes] = left[DEEP * k:DEEP * k + DEEP, :]
        for k in range(2):
            v[k, 0:DEEP, lanes] = left[360 + DEEP * k:370 + DEEP * k, :]
        fict[0:DEEP, lanes] = jnp.where(flags[2] == 1, OUTSIDE, left[380:390, :])


def lay(flags, got, z, v, fict):
    full = pl.BlockSpec(memory_space=VMEM)
    shapes = [(36, SUBS, LANES), (2, SUBS, LANES), (SUBS, LANES)]
    return pl.pallas_call(
        lay_body,
        out_shape=[jax.ShapeDtypeStruct(s, F32) for s in shapes],
        in_specs=[pl.BlockSpec(memory_space=SMEM)] + [full] * 4,
        out_specs=[full] * 3,
        input_output_aliases={2: 0, 3: 1, 4: 2},
        scratch_shapes=[VMEM((416, COLS), F32)],
        compiler_params=params(8),
        cost_estimate=work(2),
        name="lay",
    )(flags, got, z, v, fict)


def prepare_body(flags, first, heat, fictive, up, down, heat_up, heat_down, mine, side, inv_ref, half_ref, f_out, heat_t, z, v, fict_t):
    rest = SUBS - 2 * DEEP
    top, bottom = flags[0] == 1, flags[1] == 1
    for s in range(0, PIECES, 8):
        at, to = slice(32 * s, 32 * s + 256), slice(32 * s + HALO, 32 * s + HALO + 256)
        own = fictive[at, :]
        for n in range(TICKS):
            inv_ref[n, to, :], half_ref[n, to, :], own = advance(heat[s:s + 8, n].reshape(256, COLS), own)
        f_out[at, :] = own
    fict = jnp.concatenate([jnp.where(top, OUTSIDE, up[38]), jnp.where(bottom, OUTSIDE, down[38])], axis=0)
    for n in range(TICKS):
        theta = jnp.concatenate([jnp.where(top, OUTSIDE, heat_up[n]), jnp.where(bottom, OUTSIDE, heat_down[n])], axis=0)
        inv, half, fict = advance(theta, fict)
        inv_ref[n, 0:HALO, :] = inv[:HALO]
        half_ref[n, 0:HALO, :] = half[:HALO]
        inv_ref[n, HALO + ROWS:EXT, :] = inv[HALO:]
        half_ref[n, HALO + ROWS:EXT, :] = half[HALO:]
        inv_ref[n, EXT:EXT + PAD, :] = jnp.ones((PAD, COLS), F32)
        half_ref[n, EXT:EXT + PAD, :] = jnp.ones((PAD, COLS), F32)
    last_side = corner(jnp.where(top, OUTSIDE, heat_up[TICKS]), jnp.where(bottom, OUTSIDE, heat_down[TICKS]), 1.0)
    last_mine = corner(beside_each_other(lambda n: jnp.where(top, OUTSIDE, heat_up[n]), HALO),
                       beside_each_other(lambda n: jnp.where(bottom, OUTSIDE, heat_down[n]), HALO), 1.0)
    for n in range(TICKS):
        cols = slice(DEEP * n, DEEP * n + DEEP)
        heat_t[n, 0:DEEP, 0:ROWS] = side[cols, :]
        heat_t[n, 0:DEEP, ROWS:LANES] = last_side[cols]
        heat_t[n, DEEP:2 * DEEP, 0:ROWS] = mine[cols, :]
        heat_t[n, DEEP:2 * DEEP, ROWS:LANES] = last_mine[cols]
        heat_t[n, 2 * DEEP:SUBS, :] = jnp.ones((rest, LANES), F32)
    for k in range(36):
        z[k, DEEP:2 * DEEP, :] = first[DEEP * k:DEEP * k + DEEP, :]
        z[k, 2 * DEEP:SUBS, :] = jnp.zeros((rest, LANES), F32)
    for k in range(2):
        v[k, DEEP:SUBS, :] = first[360 + 16 * k:360 + 16 * k + SUBS - DEEP, :]
    fict_t[DEEP:2 * DEEP, :] = first[392:402, :]
    fict_t[2 * DEEP:SUBS, :] = jnp.ones((rest, LANES), F32)


def prepare(flags, first, heat, fictive, up, down, heat_up, heat_down, mine, side):
    full = pl.BlockSpec(memory_space=VMEM)
    factor = (TICKS, EXT + PAD, COLS)
    shapes = [factor, factor, (ROWS, COLS), (TICKS, SUBS, LANES), (36, SUBS, LANES), (2, SUBS, LANES), (SUBS, LANES)]
    return pl.pallas_call(
        prepare_body,
        out_shape=[jax.ShapeDtypeStruct(s, F32) for s in shapes],
        in_specs=[pl.BlockSpec(memory_space=SMEM)] + [full] * 9,
        out_specs=[full] * 7,
        compiler_params=params(8),
        cost_estimate=work(5),
        name="prepare",
    )(flags, first, heat, fictive, up, down, heat_up, heat_down, mine, side)


def strip_body(flags, coef, z_in, v_in, fict_in, heat_t, nodes, z, v, q):
    v[...] = v_in[...]
    q[...] = jnp.zeros((3, SUBS, LANES), F32)

    bottom = flags[1] == 1
    inside = jnp.where(bottom & (iota((8, LANES), 1) >= ROWS) & (iota((8, LANES), 1) < LANES - HALO), 0.0, 1.0)
    sum_a = coef[24]
    nodes[...] = jnp.zeros((32, LANES), F32)
    nodes[31:32, :] = v[0, DEEP:DEEP + 1, :]
    nodes[0:1, :] = v[1, DEEP:DEEP + 1, :]

    def tick(n, fict, lo, hi):
        at, size = slice(lo, hi), hi - lo
        inv, half, fict_next = advance(heat_t[n, at], fict)
        keep = jnp.concatenate([inside] * (size // 8), axis=0)

        def grads(m):
            beside = pltpu.roll(m, size - 1, 0)
            both, diff = m + beside, beside - m
            return pltpu.roll(both, LANES - 1, 1) - both, pltpu.roll(diff, LANES - 1, 1) + diff

        u, w = v[0, at], v[1, at]
        lu, wu = grads(u)
        lw, ww = grads(w)
        now = [half * lu, half * ww, (0.5 * half) * (wu + lw)]
        delta = [q[c, at] - now[c] for c in range(3)]
        for c in range(3):
            q[c, at] = now[c]
        total = [sum_a * now[c] for c in range(3)]
        for k in range(MODES):
            kept = jnp.exp2(inv * coef[k])
            a = coef[12 + k]
            for c in range(3):
                new = kept * (z[3 * k + c, at] + a * delta[c])
                z[3 * k + c, at] = new
                total[c] = total[c] + new

        def force(lin, cross):
            a, b = lin + cross, lin - cross
            return 0.5 * ((a - pltpu.roll(b, 1, 1)) + pltpu.roll(b - pltpu.roll(a, 1, 1), 1, 0))

        u_next = (u + force(total[0], total[2])) * keep
        w_next = (w + force(total[2], total[1])) * keep
        v[0, at], v[1, at] = u_next, w_next
        nodes[pl.ds(2 * n + 1, 1), :] = u_next[DEEP - lo:DEEP - lo + 1]
        nodes[pl.ds(2 * n + 2, 1), :] = w_next[DEEP - lo:DEEP - lo + 1]
        return fict_next

    fict = lax.fori_loop(0, 5, lambda n, f: tick(n, f, 0, SUBS), fict_in[...])
    fict = lax.fori_loop(5, 8, lambda n, f: tick(n, f, 0, 16), fict[:16])
    lax.fori_loop(8, TICKS, lambda n, f: tick(n, f, 8, 16), fict[8:16])


def strip(flags, coef, z, v, fict, heat_t):
    full = pl.BlockSpec(memory_space=VMEM)
    smem = pl.BlockSpec(memory_space=SMEM)
    return pl.pallas_call(
        strip_body,
        out_shape=[jax.ShapeDtypeStruct((32, LANES), F32), jax.ShapeDtypeStruct((36, SUBS, LANES), F32)],
        in_specs=[smem, smem] + [full] * 4,
        out_specs=[full, full],
        input_output_aliases={2: 1},
        scratch_shapes=[
            VMEM((2, SUBS, LANES), F32),
            VMEM((3, SUBS, LANES), F32),
        ],
        compiler_params=params(8),
        cost_estimate=work(7),
        name="strip",
    )(flags, coef, z, v, fict, heat_t)[0]


def upright(nodes, i):
    part = nodes[:, i * COLS:(i + 1) * COLS]
    return jnp.concatenate([part[:24], jnp.zeros((COLS - 32, COLS), F32), part[24:]], axis=0).T


def edges_body(nodes, left):
    for i in range(5):
        part = upright(nodes, i)
        for n in range(TICKS):
            for c in range(2):
                moved = pltpu.roll(part, COLS - (2 * n + 1 + c), 1)
                if i < 4:
                    left[n, c, HALO + i * COLS:HALO + (i + 1) * COLS, :] = moved
                else:
                    left[n, c, HALO + ROWS:EXT, :] = moved[:HALO]
                    left[n, c, 0:HALO, :] = moved[COLS - HALO:]


def edges(nodes):
    full = pl.BlockSpec(memory_space=VMEM)
    return pl.pallas_call(
        edges_body,
        out_shape=jax.ShapeDtypeStruct((TICKS, 2, EXT, COLS), F32),
        in_specs=[full],
        out_specs=full,
        compiler_params=params(8),
        cost_estimate=work(3),
        name="edges",
    )(nodes)


def block_body(flags, coef, state, motion, up, down, inv_ref, half_ref, left, beside_t, v_out, s_out, z, v, q, h, pairs, forces, zh, sem, in_sem):
    bottom = flags[1] == 1

    def in_copy(b):
        at = pl.ds(32 * b if isinstance(b, int) else pl.multiple_of(32 * b, 32), 32)
        return pltpu.make_async_copy(state.at[:, at], z.at[:, at], in_sem.at[b])

    for b in range(ROWS // 32):
        in_copy(b).start()

    for k in range(36):
        zh[k, 0:HALO, :] = up[k]
        zh[k, HALO:, :] = down[k]
    for c in range(2):
        v[c, 0:HALO, :] = up[36 + c]
        v[c, HALO:HALO + ROWS, :] = motion[c]
        v[c, HALO + ROWS:EXT, :] = down[36 + c]
        v[c, EXT:, :] = jnp.zeros((32, COLS), F32)
    q[...] = jnp.zeros((3, EXT + PAD, COLS), F32)
    forces[:, 0:8, :] = jnp.zeros((4, 8, COLS), F32)
    for i in range(5):
        part = upright(beside_t, i)
        if i < 4:
            h[HALO + i * COLS:HALO + (i + 1) * COLS, :] = part
        else:
            h[HALO + ROWS:EXT, :] = part[0:HALO]
            h[0:HALO, :] = part[COLS - HALO:]
            h[EXT:, :] = jnp.zeros((32, COLS), F32)

    lane = iota((FLOW, COLS), 1)
    at_right, at_left = lane == COLS - 1, lane == 0
    sum_a = coef[24]

    def out_copy(b):
        at = pl.ds(pl.multiple_of(32 * (b - 1), 32), 32)
        return pltpu.make_async_copy(z.at[:, at], s_out.at[:, at], sem.at[b - 1])

    def flow(n, forced, paired):
        for r in range(0, EXT, FLOW):
            at, here, above = pl.ds(r, FLOW), pl.ds(r + 8, FLOW), pl.ds(r + 7, FLOW)
            m = [v[c, at, :] for c in range(2)]
            if forced:
                for c in range(2):
                    lin, cross = 2 * c, 2 * c + 1
                    straight = forces[lin, here, :] - forces[cross, above, :]
                    turned_in = pltpu.roll(forces[cross, here, :] - forces[lin, above, :], 1, 1)
                    m[c] = jnp.where(at_left, left[n, c, at, :], m[c] + 0.5 * (straight + turned_in))
                    if r + FLOW == EXT:
                        m[c] = jnp.concatenate([m[c][:FLOW - HALO], jnp.where(bottom, 0.0, m[c][FLOW - HALO:])], axis=0)
                    v[c, at, :] = m[c]
            if paired:
                hist = h[at, :]
                h[at, :] = pltpu.roll(hist, COLS - 2, 1)
                beside = (jnp.where(at_right, hist, pltpu.roll(m[0], COLS - 1, 1)),
                          pltpu.roll(jnp.where(at_left, hist, m[1]), COLS - 1, 1))
                for c in range(2):
                    pairs[2 * c, at, :] = m[c] + beside[c]
                    pairs[2 * c + 1, at, :] = beside[c] - m[c]

    def relax(n, r, zs, r_z, size, final):
        at, below, at_z = pl.ds(r, size), pl.ds(r + 1, size), pl.ds(r_z, size)
        along = [pairs[2 * c, below, :] - pairs[2 * c, at, :] for c in range(2)]
        across = [pairs[2 * c + 1, below, :] + pairs[2 * c + 1, at, :] for c in range(2)]
        half, inv = half_ref[n, at, :], inv_ref[n, at, :]
        now = [half * along[0], half * across[1], (0.5 * half) * (across[0] + along[1])]
        delta = [q[c, at, :] - now[c] for c in range(3)]
        for c in range(3):
            q[c, at, :] = now[c]
        total = [sum_a * x for x in now]
        for k in range(MODES):
            kept = jnp.exp2(inv * coef[k])
            a = coef[12 + k]
            for c in range(3):
                new = kept * (zs[3 * k + c, at_z, :] + a * delta[c])
                zs[3 * k + c, at_z, :] = (new + a * now[c]) if final else new
                total[c] = total[c] + new
        xx, yy, xy = total
        for i, part in enumerate((xx + xy, xx - xy, xy + yy, xy - yy)):
            forces[i, pl.ds(r + 8, size), :] = part

    def relax_group(n, b, final):
        fixed = isinstance(b, int)
        size = HALO if fixed else SUB
        for t in range(0, 32, size):
            r = 32 * b + t
            if not fixed:
                r = pl.multiple_of(r, 8)
            if fixed and b == 0 and t < HALO:
                relax(n, r, zh, t, size, final)
            elif fixed and b > 0 and t >= HALO:
                relax(n, r, zh, t, size, final)
            else:
                relax(n, r, z, r - HALO, size, final)

    def tick(n, starting, final):
        if starting:
            in_copy(0).wait()
        relax_group(n, 0, final)

        def body(i, _):
            for j in range(SPAN):
                b = SPAN * i + j + 1
                if starting:
                    in_copy(b).wait()
                relax_group(n, b, final)
                if final:
                    out_copy(b).start()
            return 0

        last = EXT // 32 - 1
        lax.fori_loop(0, (last - 1) // SPAN, body, 0)
        relax_group(n, last, final)
        if final:
            out_copy(last).start()
        flow(n, True, not final)

    def step(n, _):
        tick(n, False, False)
        return 0

    flow(0, False, True)
    tick(0, True, False)
    lax.fori_loop(1, TICKS - 1, step, 0)
    tick(TICKS - 1, False, True)
    for c in range(2):
        v_out[c] = v[c, HALO:HALO + ROWS, :]
    for b in range(1, EXT // 32):
        out_copy(b).wait()


def block(flags, coef, state, motion, up, down, inv, half, left, beside):
    full = pl.BlockSpec(memory_space=VMEM)
    smem = pl.BlockSpec(memory_space=SMEM)
    return pl.pallas_call(
        block_body,
        out_shape=[
            jax.ShapeDtypeStruct((2, ROWS, COLS), F32),
            pltpu.HBM((36, ROWS, COLS), F32),
        ],
        in_specs=[smem, smem, pl.BlockSpec(memory_space=pltpu.HBM)] + [full] * 7,
        out_specs=[full, pl.BlockSpec(memory_space=pltpu.HBM)],
        scratch_shapes=[
            VMEM((36, ROWS, COLS), F32),
            VMEM((2, EXT + 32, COLS), F32),
            VMEM((3, EXT + PAD, COLS), F32),
            VMEM((EXT + 32, COLS), F32),
            VMEM((4, EXT + 32, COLS), F32),
            VMEM((4, EXT + 8, COLS), F32),
            VMEM((36, 2 * HALO, COLS), F32),
            pltpu.SemaphoreType.DMA((EXT // 32 - 1,)),
            pltpu.SemaphoreType.DMA((ROWS // 32,)),
        ],
        compiler_params=params(26),
        cost_estimate=work(28),
        name="block",
    )(flags, coef, pinned(state), motion, up, down, inv, half, left, beside)


def shards(warmth_history, fictitious_warmth, vertex_velocity, branch_load_tensors, mechanism_lifetimes, branch_stiffness):
    state = branch_load_tensors.reshape(3 * MODES, ROWS, COLS)
    weight = 2.0 * branch_stiffness * mechanism_lifetimes
    coef = jnp.concatenate([-LOG2E / mechanism_lifetimes, weight, jnp.sum(weight)[None]])
    draw, wide = lax.axis_index("draw"), lax.axis_index(WIDE)
    flags = jnp.stack([draw == 0, draw == lax.axis_size("draw") - 1, wide == 0]).astype(jnp.int32)

    slab, above, below = cut(warmth_history, state, vertex_velocity, fictitious_warmth)
    heat = lax.all_to_all(slab, WIDE, split_axis=0, concat_axis=0, tiled=True)
    up = shifted(above, "draw", 1)
    down = shifted(below, "draw", -1)
    up, down, coef = lax.optimization_barrier((up, down, coef))
    first, final = pack(flags, state, vertex_velocity, fictitious_warmth, up, down)
    got = shifted(final, WIDE, 1)
    heat_up = shifted(heat[PIECES - 1, :, HALO:, :], "draw", 1)
    heat_down = shifted(heat[0, :, :HALO, :], "draw", -1)
    mine, side = ready(heat)
    inv, half, fict, heat_t, z, v, fict_t = prepare(flags, first, heat, fictitious_warmth, up, down, heat_up, heat_down, mine, side)
    got, fict_t = lax.optimization_barrier((got, fict_t))
    nodes = strip(flags, coef, *lay(flags, got, z, v, fict_t), heat_t)
    beside = shifted(nodes, WIDE, -1)
    left = edges(nodes)
    motion, modes = block(flags, coef, state, vertex_velocity, up, down, inv, half, left, beside)
    return fict, motion, modes.reshape(branch_load_tensors.shape)


def solution(mesh):
    in_specs = (
        P(None, ("draw", "width", "cores"), None),
        P("draw", ("width", "cores")),
        P(None, "draw", ("width", "cores")),
        P(None, None, "draw", ("width", "cores")),
        P(),
        P(),
    )
    out_specs = (
        P("draw", ("width", "cores")),
        P(None, "draw", ("width", "cores")),
        P(None, None, "draw", ("width", "cores")),
    )
    return jax.shard_map(shards, mesh=mesh, in_specs=in_specs, out_specs=out_specs, check_vma=False)
```

```python
import jax
import jax.numpy as jnp
from jax import lax
from jax.experimental import pallas as pl
from jax.experimental.pallas import tpu as pltpu
from jax.sharding import PartitionSpec as P

LOG2E = 1.4426950408889634
OUTSIDE = -1.0 / 3.0
TICKS = 10
MODES = 12
PIECES = 16
ROWS = 512
COLS = 128
HALO = 16
EXT = ROWS + 2 * HALO
DEEP = 10
LANES = 640
SUBS = 24
PAD = 8
EDGE = 392
SPAN = 3
SUB = 16
FLOW = 272
F32 = jnp.float32
VMEM = pltpu.VMEM
ANY = pl.ANY
SMEM = pltpu.SMEM
WIDE = ("width", "cores")


def shifted(shard, axis, by):
    peers = lax.axis_size(axis)
    pairs = [(i, i + by) for i in range(peers) if 0 <= i + by < peers]
    return lax.ppermute(shard, axis, pairs)


def params(mb):
    return pltpu.CompilerParams(vmem_limit_bytes=mb << 20)


def iota(shape, axis):
    return lax.broadcasted_iota(jnp.int32, shape, axis)


def pinned(x):
    return pltpu.with_memory_space_constraint(x, pltpu.HBM)


def cut_body(src, state, motion, fictive, dst, above, below, buf, side, halo, in_sem, out_sem, side_sem, row_sem):
    def fetch(p):
        return pltpu.make_async_copy(src.at[:, :, pl.ds(p * COLS, COLS)], buf.at[p], in_sem.at[p])

    def put(p):
        return pltpu.make_async_copy(buf.at[p], dst.at[p, pl.ds(0, TICKS)], out_sem.at[p])

    def put_side(p):
        return pltpu.make_async_copy(side.at[p], dst.at[p, TICKS], side_sem.at[p])

    ins, outs = [], []
    for i, (to, at) in enumerate(((above, ROWS - HALO), (below, 0))):
        part = pl.ds(at, HALO)
        for x, y in ((state.at[:, part], pl.ds(0, 36)), (motion.at[:, part], pl.ds(36, 2)), (fictive.at[part], 38)):
            ins.append(pltpu.make_async_copy(x, halo.at[i, y], row_sem.at[len(ins)]))
        outs.append(pltpu.make_async_copy(halo.at[i], to, row_sem.at[6 + i]))
    for p in range(PIECES):
        fetch(p).start()
    for c in ins:
        c.start()
    lane = iota((32, COLS), 1)
    for p in range(PIECES):
        fetch(p).wait()
        put(p).start()
        if p == 0:
            side[0] = jnp.full((32, COLS), OUTSIDE, F32)
            put_side(0).start()
        if p + 1 < PIECES:
            acc = jnp.full((32, COLS), 1.0, F32)
            for n in range(TICKS):
                moved = pltpu.roll(buf[p, n], (DEEP * n + DEEP) % COLS, 1)
                acc = jnp.where((lane >= DEEP * n) & (lane < DEEP * n + DEEP), moved, acc)
            side[p + 1] = acc
            put_side(p + 1).start()
    for c in ins:
        c.wait()
    for c in outs:
        c.start()
    for p in range(PIECES):
        put(p).wait()
        put_side(p).wait()
    for c in outs:
        c.wait()


def cut(slab, state, motion, fictive):
    hbm = pl.BlockSpec(memory_space=pltpu.HBM)
    halo = pltpu.HBM((39, HALO, COLS), F32)
    return pl.pallas_call(
        cut_body,
        out_shape=[pltpu.HBM((PIECES, TICKS + 1, 32, COLS), F32), halo, halo],
        in_specs=[hbm] * 4,
        out_specs=[hbm] * 3,
        scratch_shapes=[
            VMEM((PIECES, TICKS, 32, COLS), F32),
            VMEM((PIECES, 32, COLS), F32),
            VMEM((2, 39, HALO, COLS), F32),
            pltpu.SemaphoreType.DMA((PIECES,)),
            pltpu.SemaphoreType.DMA((PIECES,)),
            pltpu.SemaphoreType.DMA((PIECES,)),
            pltpu.SemaphoreType.DMA((8,)),
        ],
        compiler_params=params(8),
        name="cut",
    )(pinned(slab), pinned(state), pinned(motion), pinned(fictive))


def corner(up, down, fill):
    return jnp.concatenate([down, jnp.full((COLS - 2 * HALO, COLS), fill, F32), up], axis=0).T


def turned(own):
    return jnp.concatenate([own[i * COLS:(i + 1) * COLS].T for i in range(4)], axis=1)


def pack_body(flags, state, motion, fictive, up, down, first_out, send, buf, tail, first, more, sem, more_sem):
    copies = [pltpu.make_async_copy(state.at[pl.ds(4 * i, 4)], buf.at[pl.ds(4 * i, 4)], sem.at[i]) for i in range(9)]
    rest = [pltpu.make_async_copy(motion, more.at[pl.ds(0, 2)], more_sem.at[0]), pltpu.make_async_copy(fictive, more.at[2], more_sem.at[1])]
    for c in copies + rest:
        c.start()

    def put(at, blocks, corners, widths):
        for i in range(5):
            parts = corners if i == 4 else [b[i * COLS:(i + 1) * COLS].T for b in blocks]
            lanes = slice(i * COLS, (i + 1) * COLS)
            own = jnp.concatenate([p[:w] for p, w in zip(parts, widths)], axis=0)
            first[at:at + own.shape[0], lanes] = own
            gone = [p[COLS - DEEP:] for p in parts]
            if len(gone) == 3:
                gone.append(jnp.zeros((2, COLS), F32))
            gone = jnp.concatenate(gone, axis=0)
            if i < 4:
                send[EDGE * i + at:EDGE * i + at + gone.shape[0], :] = gone
            else:
                tail[at:at + gone.shape[0], :] = gone

    f_up = jnp.where(flags[0] == 1, OUTSIDE, up[38])
    f_down = jnp.where(flags[1] == 1, OUTSIDE, down[38])
    for i in range(9):
        copies[i].wait()
        put(40 * i, [buf[4 * i + j] for j in range(4)], [corner(up[4 * i + j], down[4 * i + j], 0.0) for j in range(4)], (DEEP,) * 4)
    for c in rest:
        c.wait()
    put(360, [more[0], more[1], more[2]], [corner(up[36], down[36], 0.0), corner(up[37], down[37], 0.0), corner(f_up, f_down, 1.0)], (16, 16, 16))
    keep = pltpu.make_async_copy(first, first_out, more_sem.at[2])
    keep.start()
    tail[EDGE:416, :] = jnp.zeros((416 - EDGE, COLS), F32)
    lane = iota((104, COLS), 1)
    acc = jnp.zeros((104, COLS), F32)
    for j in range(4):
        moved = pltpu.roll(tail[104 * j:104 * j + 104, :], (HALO + 32 * j) % COLS, 1)
        acc = jnp.where((lane >= 32 * j) & (lane < 32 * j + 32), moved, acc)
    send[4 * EDGE:, :] = acc
    keep.wait()


def spread(dense):
    return jnp.concatenate([pltpu.roll(dense, COLS - HALO - 32 * j, 1) for j in range(4)], axis=0)


def pack(flags, state, motion, fictive, up, down):
    full = pl.BlockSpec(memory_space=VMEM)
    hbm = pl.BlockSpec(memory_space=pltpu.HBM)
    return pl.pallas_call(
        pack_body,
        out_shape=[pltpu.HBM((408, LANES), F32), jax.ShapeDtypeStruct((4 * EDGE + 104, COLS), F32)],
        in_specs=[pl.BlockSpec(memory_space=SMEM)] + [hbm] * 3 + [full] * 2,
        out_specs=[hbm, full],
        scratch_shapes=[
            VMEM((36, ROWS, COLS), F32),
            VMEM((416, COLS), F32),
            VMEM((408, LANES), F32),
            VMEM((3, ROWS, COLS), F32),
            pltpu.SemaphoreType.DMA((9,)),
            pltpu.SemaphoreType.DMA((3,)),
        ],
        compiler_params=params(20),
        name="pack",
    )(flags, pinned(state), pinned(motion), pinned(fictive), up, down)


def shift_of(theta, fict):
    arg = 10.0 * (theta + fict) / (theta * fict) - 20.0
    inv = jnp.exp(-arg)
    return inv, jnp.exp(arg)


def work(us):
    return pl.CostEstimate(flops=0, transcendentals=0, bytes_accessed=us * 3_000_000)


def beside_each_other(pick, rows):
    lane = iota((rows, COLS), 1)
    acc = jnp.full((rows, COLS), 1.0, F32)
    for n in range(TICKS):
        moved = pltpu.roll(pick(n), DEEP * n, 1) if n else pick(n)
        acc = jnp.where((lane >= DEEP * n) & (lane < DEEP * n + DEEP), moved, acc)
    return acc


def advance(theta, fict):
    inv, shift = shift_of(theta, fict)
    return inv, 0.5 * shift, theta + (fict - theta) * jnp.exp(inv * (-1.0 / 3.0))


def ready_body(heat, mine, side):
    own = jnp.concatenate([beside_each_other(lambda n: heat[s, n], 32) for s in range(PIECES)], axis=0)
    mine[...] = turned(own)
    side[...] = turned(jnp.concatenate([heat[s, TICKS] for s in range(PIECES)], axis=0))


def ready(heat):
    full = pl.BlockSpec(memory_space=VMEM)
    row_t = jax.ShapeDtypeStruct((COLS, ROWS), F32)
    return pl.pallas_call(
        ready_body,
        out_shape=[row_t, row_t],
        in_specs=[full],
        out_specs=[full] * 2,
        compiler_params=params(8),
        cost_estimate=work(3),
        name="ready",
    )(heat)


def lay_body(flags, got, z_in, v_in, fict_in, z, v, fict, got_halo):
    lane = iota((416, COLS), 1)
    blank = jnp.where((iota((416, COLS), 0) >= 380) & (iota((416, COLS), 0) < 390), 1.0, 0.0)
    got_halo[...] = jnp.where((lane < HALO) | (lane >= COLS - HALO), spread(got[4 * EDGE:, :]), blank)
    for i in range(5):
        lanes = slice(i * COLS, (i + 1) * COLS)
        left = got_halo if i == 4 else got.at[pl.ds(EDGE * i, EDGE)]
        for k in range(36):
            z[k, 0:DEEP, lanes] = left[DEEP * k:DEEP * k + DEEP, :]
        for k in range(2):
            v[k, 0:DEEP, lanes] = left[360 + DEEP * k:370 + DEEP * k, :]
        fict[0:DEEP, lanes] = jnp.where(flags[2] == 1, OUTSIDE, left[380:390, :])


def lay(flags, got, z, v, fict):
    full = pl.BlockSpec(memory_space=VMEM)
    shapes = [(36, SUBS, LANES), (2, SUBS, LANES), (SUBS, LANES)]
    return pl.pallas_call(
        lay_body,
        out_shape=[jax.ShapeDtypeStruct(s, F32) for s in shapes],
        in_specs=[pl.BlockSpec(memory_space=SMEM)] + [full] * 4,
        out_specs=[full] * 3,
        input_output_aliases={2: 0, 3: 1, 4: 2},
        scratch_shapes=[VMEM((416, COLS), F32)],
        compiler_params=params(8),
        cost_estimate=work(2),
        name="lay",
    )(flags, got, z, v, fict)


def prepare_body(flags, first, heat, fictive, up, down, heat_up, heat_down, mine, side, inv_ref, half_ref, f_out, heat_t, z, v, fict_t):
    rest = SUBS - 2 * DEEP
    top, bottom = flags[0] == 1, flags[1] == 1
    for s in range(0, PIECES, 8):
        at, to = slice(32 * s, 32 * s + 256), slice(32 * s + HALO, 32 * s + HALO + 256)
        own = fictive[at, :]
        for n in range(TICKS):
            inv_ref[n, to, :], half_ref[n, to, :], own = advance(heat[s:s + 8, n].reshape(256, COLS), own)
        f_out[at, :] = own
    fict = jnp.concatenate([jnp.where(top, OUTSIDE, up[38]), jnp.where(bottom, OUTSIDE, down[38])], axis=0)
    for n in range(TICKS):
        theta = jnp.concatenate([jnp.where(top, OUTSIDE, heat_up[n]), jnp.where(bottom, OUTSIDE, heat_down[n])], axis=0)
        inv, half, fict = advance(theta, fict)
        inv_ref[n, 0:HALO, :] = inv[:HALO]
        half_ref[n, 0:HALO, :] = half[:HALO]
        inv_ref[n, HALO + ROWS:EXT, :] = inv[HALO:]
        half_ref[n, HALO + ROWS:EXT, :] = half[HALO:]
        inv_ref[n, EXT:EXT + PAD, :] = jnp.ones((PAD, COLS), F32)
        half_ref[n, EXT:EXT + PAD, :] = jnp.ones((PAD, COLS), F32)
    last_side = corner(jnp.where(top, OUTSIDE, heat_up[TICKS]), jnp.where(bottom, OUTSIDE, heat_down[TICKS]), 1.0)
    last_mine = corner(beside_each_other(lambda n: jnp.where(top, OUTSIDE, heat_up[n]), HALO),
                       beside_each_other(lambda n: jnp.where(bottom, OUTSIDE, heat_down[n]), HALO), 1.0)
    for n in range(TICKS):
        cols = slice(DEEP * n, DEEP * n + DEEP)
        heat_t[n, 0:DEEP, 0:ROWS] = side[cols, :]
        heat_t[n, 0:DEEP, ROWS:LANES] = last_side[cols]
        heat_t[n, DEEP:2 * DEEP, 0:ROWS] = mine[cols, :]
        heat_t[n, DEEP:2 * DEEP, ROWS:LANES] = last_mine[cols]
        heat_t[n, 2 * DEEP:SUBS, :] = jnp.ones((rest, LANES), F32)
    for k in range(36):
        z[k, DEEP:2 * DEEP, :] = first[DEEP * k:DEEP * k + DEEP, :]
        z[k, 2 * DEEP:SUBS, :] = jnp.zeros((rest, LANES), F32)
    for k in range(2):
        v[k, DEEP:SUBS, :] = first[360 + 16 * k:360 + 16 * k + SUBS - DEEP, :]
    fict_t[DEEP:2 * DEEP, :] = first[392:402, :]
    fict_t[2 * DEEP:SUBS, :] = jnp.ones((rest, LANES), F32)


def prepare(flags, first, heat, fictive, up, down, heat_up, heat_down, mine, side):
    full = pl.BlockSpec(memory_space=VMEM)
    factor = (TICKS, EXT + PAD, COLS)
    shapes = [factor, factor, (ROWS, COLS), (TICKS, SUBS, LANES), (36, SUBS, LANES), (2, SUBS, LANES), (SUBS, LANES)]
    return pl.pallas_call(
        prepare_body,
        out_shape=[jax.ShapeDtypeStruct(s, F32) for s in shapes],
        in_specs=[pl.BlockSpec(memory_space=SMEM)] + [full] * 9,
        out_specs=[full] * 7,
        compiler_params=params(8),
        cost_estimate=work(5),
        name="prepare",
    )(flags, first, heat, fictive, up, down, heat_up, heat_down, mine, side)


def strip_body(flags, coef, z_in, v_in, fict_in, heat_t, nodes, z, v, q):
    v[...] = v_in[...]
    q[...] = jnp.zeros((3, SUBS, LANES), F32)

    bottom = flags[1] == 1
    inside = jnp.where(bottom & (iota((8, LANES), 1) >= ROWS) & (iota((8, LANES), 1) < LANES - HALO), 0.0, 1.0)
    sum_a = coef[24]
    nodes[...] = jnp.zeros((32, LANES), F32)
    nodes[31:32, :] = v[0, DEEP:DEEP + 1, :]
    nodes[0:1, :] = v[1, DEEP:DEEP + 1, :]

    def tick(n, fict, lo, hi):
        at, size = slice(lo, hi), hi - lo
        inv, half, fict_next = advance(heat_t[n, at], fict)
        keep = jnp.concatenate([inside] * (size // 8), axis=0)

        def grads(m):
            beside = pltpu.roll(m, size - 1, 0)
            both, diff = m + beside, beside - m
            return pltpu.roll(both, LANES - 1, 1) - both, pltpu.roll(diff, LANES - 1, 1) + diff

        u, w = v[0, at], v[1, at]
        lu, wu = grads(u)
        lw, ww = grads(w)
        now = [half * lu, half * ww, (0.5 * half) * (wu + lw)]
        delta = [q[c, at] - now[c] for c in range(3)]
        for c in range(3):
            q[c, at] = now[c]
        total = [sum_a * now[c] for c in range(3)]
        for k in range(MODES):
            kept = jnp.exp2(inv * coef[k])
            a = coef[12 + k]
            for c in range(3):
                new = kept * (z[3 * k + c, at] + a * delta[c])
                z[3 * k + c, at] = new
                total[c] = total[c] + new

        def force(lin, cross):
            a, b = lin + cross, lin - cross
            return 0.5 * ((a - pltpu.roll(b, 1, 1)) + pltpu.roll(b - pltpu.roll(a, 1, 1), 1, 0))

        u_next = (u + force(total[0], total[2])) * keep
        w_next = (w + force(total[2], total[1])) * keep
        v[0, at], v[1, at] = u_next, w_next
        nodes[pl.ds(2 * n + 1, 1), :] = u_next[DEEP - lo:DEEP - lo + 1]
        nodes[pl.ds(2 * n + 2, 1), :] = w_next[DEEP - lo:DEEP - lo + 1]
        return fict_next

    fict = lax.fori_loop(0, 5, lambda n, f: tick(n, f, 0, SUBS), fict_in[...])
    fict = lax.fori_loop(5, 8, lambda n, f: tick(n, f, 0, 16), fict[:16])
    lax.fori_loop(8, TICKS, lambda n, f: tick(n, f, 8, 16), fict[8:16])


def strip(flags, coef, z, v, fict, heat_t):
    full = pl.BlockSpec(memory_space=VMEM)
    smem = pl.BlockSpec(memory_space=SMEM)
    return pl.pallas_call(
        strip_body,
        out_shape=[jax.ShapeDtypeStruct((32, LANES), F32), jax.ShapeDtypeStruct((36, SUBS, LANES), F32)],
        in_specs=[smem, smem] + [full] * 4,
        out_specs=[full, full],
        input_output_aliases={2: 1},
        scratch_shapes=[
            VMEM((2, SUBS, LANES), F32),
            VMEM((3, SUBS, LANES), F32),
        ],
        compiler_params=params(8),
        cost_estimate=work(7),
        name="strip",
    )(flags, coef, z, v, fict, heat_t)[0]


def upright(nodes, i):
    part = nodes[:, i * COLS:(i + 1) * COLS]
    return jnp.concatenate([part[:24], jnp.zeros((COLS - 32, COLS), F32), part[24:]], axis=0).T


def edges_body(nodes, left):
    for i in range(5):
        part = upright(nodes, i)
        for n in range(TICKS):
            for c in range(2):
                moved = pltpu.roll(part, COLS - (2 * n + 1 + c), 1)
                if i < 4:
                    left[n, c, HALO + i * COLS:HALO + (i + 1) * COLS, :] = moved
                else:
                    left[n, c, HALO + ROWS:EXT, :] = moved[:HALO]
                    left[n, c, 0:HALO, :] = moved[COLS - HALO:]


def edges(nodes):
    full = pl.BlockSpec(memory_space=VMEM)
    return pl.pallas_call(
        edges_body,
        out_shape=jax.ShapeDtypeStruct((TICKS, 2, EXT, COLS), F32),
        in_specs=[full],
        out_specs=full,
        compiler_params=params(8),
        cost_estimate=work(3),
        name="edges",
    )(nodes)


def block_body(flags, coef, state, motion, up, down, inv_ref, half_ref, left, beside_t, v_out, s_out, z, v, q, h, pairs, forces, zh, sem, in_sem):
    bottom = flags[1] == 1

    def in_copy(b):
        at = pl.ds(32 * b if isinstance(b, int) else pl.multiple_of(32 * b, 32), 32)
        return pltpu.make_async_copy(state.at[:, at], z.at[:, at], in_sem.at[b])

    for b in range(ROWS // 32):
        in_copy(b).start()

    for k in range(36):
        zh[k, 0:HALO, :] = up[k]
        zh[k, HALO:, :] = down[k]
    for c in range(2):
        v[c, 0:HALO, :] = up[36 + c]
        v[c, HALO:HALO + ROWS, :] = motion[c]
        v[c, HALO + ROWS:EXT, :] = down[36 + c]
        v[c, EXT:, :] = jnp.zeros((32, COLS), F32)
    q[...] = jnp.zeros((3, EXT + PAD, COLS), F32)
    forces[:, 0:8, :] = jnp.zeros((4, 8, COLS), F32)
    for i in range(5):
        part = upright(beside_t, i)
        if i < 4:
            h[HALO + i * COLS:HALO + (i + 1) * COLS, :] = part
        else:
            h[HALO + ROWS:EXT, :] = part[0:HALO]
            h[0:HALO, :] = part[COLS - HALO:]
            h[EXT:, :] = jnp.zeros((32, COLS), F32)

    lane = iota((FLOW, COLS), 1)
    at_right, at_left = lane == COLS - 1, lane == 0
    sum_a = coef[24]

    def out_copy(b):
        at = pl.ds(pl.multiple_of(32 * (b - 1), 32), 32)
        return pltpu.make_async_copy(z.at[:, at], s_out.at[:, at], sem.at[b - 1])

    def flow(n, forced, paired):
        for r in range(0, EXT, FLOW):
            at, here, above = pl.ds(r, FLOW), pl.ds(r + 8, FLOW), pl.ds(r + 7, FLOW)
            m = [v[c, at, :] for c in range(2)]
            if forced:
                for c in range(2):
                    lin, cross = 2 * c, 2 * c + 1
                    straight = forces[lin, here, :] - forces[cross, above, :]
                    turned_in = pltpu.roll(forces[cross, here, :] - forces[lin, above, :], 1, 1)
                    m[c] = jnp.where(at_left, left[n, c, at, :], m[c] + 0.5 * (straight + turned_in))
                    if r + FLOW == EXT:
                        m[c] = jnp.concatenate([m[c][:FLOW - HALO], jnp.where(bottom, 0.0, m[c][FLOW - HALO:])], axis=0)
                    v[c, at, :] = m[c]
            if paired:
                hist = h[at, :]
                h[at, :] = pltpu.roll(hist, COLS - 2, 1)
                beside = (jnp.where(at_right, hist, pltpu.roll(m[0], COLS - 1, 1)),
                          pltpu.roll(jnp.where(at_left, hist, m[1]), COLS - 1, 1))
                for c in range(2):
                    pairs[2 * c, at, :] = m[c] + beside[c]
                    pairs[2 * c + 1, at, :] = beside[c] - m[c]

    def relax(n, r, zs, r_z, size, final):
        at, below, at_z = pl.ds(r, size), pl.ds(r + 1, size), pl.ds(r_z, size)
        along = [pairs[2 * c, below, :] - pairs[2 * c, at, :] for c in range(2)]
        across = [pairs[2 * c + 1, below, :] + pairs[2 * c + 1, at, :] for c in range(2)]
        half, inv = half_ref[n, at, :], inv_ref[n, at, :]
        now = [half * along[0], half * across[1], (0.5 * half) * (across[0] + along[1])]
        delta = [q[c, at, :] - now[c] for c in range(3)]
        for c in range(3):
            q[c, at, :] = now[c]
        total = [sum_a * x for x in now]
        for k in range(MODES):
            kept = jnp.exp2(inv * coef[k])
            a = coef[12 + k]
            for c in range(3):
                new = kept * (zs[3 * k + c, at_z, :] + a * delta[c])
                zs[3 * k + c, at_z, :] = (new + a * now[c]) if final else new
                total[c] = total[c] + new
        xx, yy, xy = total
        for i, part in enumerate((xx + xy, xx - xy, xy + yy, xy - yy)):
            forces[i, pl.ds(r + 8, size), :] = part

    def relax_group(n, b, final):
        fixed = isinstance(b, int)
        size = HALO if fixed else SUB
        for t in range(0, 32, size):
            r = 32 * b + t
            if not fixed:
                r = pl.multiple_of(r, 8)
            if fixed and b == 0 and t < HALO:
                relax(n, r, zh, t, size, final)
            elif fixed and b > 0 and t >= HALO:
                relax(n, r, zh, t, size, final)
            else:
                relax(n, r, z, r - HALO, size, final)

    def tick(n, starting, final):
        if starting:
            in_copy(0).wait()
        relax_group(n, 0, final)

        def body(i, _):
            for j in range(SPAN):
                b = SPAN * i + j + 1
                if starting:
                    in_copy(b).wait()
                relax_group(n, b, final)
                if final:
                    out_copy(b).start()
            return 0

        last = EXT // 32 - 1
        lax.fori_loop(0, (last - 1) // SPAN, body, 0)
        relax_group(n, last, final)
        if final:
            out_copy(last).start()
        flow(n, True, not final)

    def step(n, _):
        tick(n, False, False)
        return 0

    flow(0, False, True)
    tick(0, True, False)
    lax.fori_loop(1, TICKS - 1, step, 0)
    tick(TICKS - 1, False, True)
    for c in range(2):
        v_out[c] = v[c, HALO:HALO + ROWS, :]
    for b in range(1, EXT // 32):
        out_copy(b).wait()


def block(flags, coef, state, motion, up, down, inv, half, left, beside):
    full = pl.BlockSpec(memory_space=VMEM)
    smem = pl.BlockSpec(memory_space=SMEM)
    return pl.pallas_call(
        block_body,
        out_shape=[
            jax.ShapeDtypeStruct((2, ROWS, COLS), F32),
            pltpu.HBM((36, ROWS, COLS), F32),
        ],
        in_specs=[smem, smem, pl.BlockSpec(memory_space=pltpu.HBM)] + [full] * 7,
        out_specs=[full, pl.BlockSpec(memory_space=pltpu.HBM)],
        scratch_shapes=[
            VMEM((36, ROWS, COLS), F32),
            VMEM((2, EXT + 32, COLS), F32),
            VMEM((3, EXT + PAD, COLS), F32),
            VMEM((EXT + 32, COLS), F32),
            VMEM((4, EXT + 32, COLS), F32),
            VMEM((4, EXT + 8, COLS), F32),
            VMEM((36, 2 * HALO, COLS), F32),
            pltpu.SemaphoreType.DMA((EXT // 32 - 1,)),
            pltpu.SemaphoreType.DMA((ROWS // 32,)),
        ],
        compiler_params=params(26),
        cost_estimate=work(28),
        name="block",
    )(flags, coef, pinned(state), motion, up, down, inv, half, left, beside)


def shards(warmth_history, fictitious_warmth, vertex_velocity, branch_load_tensors, mechanism_lifetimes, branch_stiffness):
    state = branch_load_tensors.reshape(3 * MODES, ROWS, COLS)
    weight = 2.0 * branch_stiffness * mechanism_lifetimes
    coef = jnp.concatenate([-LOG2E / mechanism_lifetimes, weight, jnp.sum(weight)[None]])
    draw, wide = lax.axis_index("draw"), lax.axis_index(WIDE)
    flags = jnp.stack([draw == 0, draw == lax.axis_size("draw") - 1, wide == 0]).astype(jnp.int32)

    slab, above, below = cut(warmth_history, state, vertex_velocity, fictitious_warmth)
    heat = lax.all_to_all(slab, WIDE, split_axis=0, concat_axis=0, tiled=True)
    up = shifted(above, "draw", 1)
    down = shifted(below, "draw", -1)
    up, down, coef = lax.optimization_barrier((up, down, coef))
    first, final = pack(flags, state, vertex_velocity, fictitious_warmth, up, down)
    got = shifted(final, WIDE, 1)
    heat_up = shifted(heat[PIECES - 1, :, HALO:, :], "draw", 1)
    heat_down = shifted(heat[0, :, :HALO, :], "draw", -1)
    mine, side = ready(heat)
    inv, half, fict, heat_t, z, v, fict_t = prepare(flags, first, heat, fictitious_warmth, up, down, heat_up, heat_down, mine, side)
    got, fict_t = lax.optimization_barrier((got, fict_t))
    nodes = strip(flags, coef, *lay(flags, got, z, v, fict_t), heat_t)
    beside = shifted(nodes, WIDE, -1)
    left = edges(nodes)
    motion, modes = block(flags, coef, state, vertex_velocity, up, down, inv, half, left, beside)
    return fict, motion, modes.reshape(branch_load_tensors.shape)


def solution(mesh):
    in_specs = (
        P(None, ("draw", "width", "cores"), None),
        P("draw", ("width", "cores")),
        P(None, "draw", ("width", "cores")),
        P(None, None, "draw", ("width", "cores")),
        P(),
        P(),
    )
    out_specs = (
        P("draw", ("width", "cores")),
        P(None, "draw", ("width", "cores")),
        P(None, None, "draw", ("width", "cores")),
    )
    return jax.shard_map(shards, mesh=mesh, in_specs=in_specs, out_specs=out_specs, check_vma=False)
```
